256 devices in a mesh: tm: 8 (over y_lo, x), space: 32 (over y_hi, z, core).
Axes of the slice: x: 4, y: 4 (y_hi: 2, y_lo: 2; y = y_hi * 2 + y_lo), z: 8, core: 2. Of those that a mesh axis runs over, the one named last changes fastest.
Arguments:
- hidden_in: bfloat16 [16, 64, 32, 5120], P('tm', 'space'), may hold values from -6 to 6
- queries: bfloat16 [16, 64, 32, 5120], P('tm', 'space'), may hold values from -250 to 250
- keys: bfloat16 [16, 64, 32, 5120], P('tm', 'space'), may hold values from -250 to 250
- values: bfloat16 [16, 64, 32, 5120], P('tm', 'space'), may hold values from -6 to 6
- query_gain: float32 [5120], replicated, may hold values from 0.5 to 3
- key_gain: float32 [5120], replicated, may hold values from 0.5 to 3
- reach_time: int32 [40], replicated, may hold values from 0 to 1
- reach_rows: int32 [40], replicated, may hold values from 0 to 1
- reach_cols: int32 [40], replicated, may hold values from 0 to 2
- out_weight: bfloat16 [5120, 5120], P('space', 'tm'), may hold values from -0.25 to 0.25
- gate: float32 [5120], replicated, may hold values from -1.5 to 1.5
Outputs:
- output: bfloat16 [16, 64, 32, 5120], P('tm', 'space')
The draws below stay inside these ranges and needn't reach their ends.
All inputs are finite; a program needn't handle non-finite values.
Results may differ from the reference program's by a relative error of at most 0.013.
The reference program's roundings to bfloat16 on the way (of `query_norm`, `key_norm`, `rounded` and `attention`) count: a program that leaves them out, or rounds other values in their place, can miss the bound.
Values may be sent and summed in bfloat16 or wider, within the bound.
No kernel may reach another device: no remote copies, remote signals or barrier semaphores. Data moves between devices by JAX's collectives and lax.ppermute only.
A program may use at most 128 MiB of HBM per device.

```python
import math
import jax
import jax.numpy as jnp
from jax import lax

D = 5120
HEADS = 40
FR = 2
RH = 2
NW = 32
TW = 8
INNER = 5120
NF = 16
NH = 64


def lifted_field(key, salt):
    base = jax.random.normal(jax.random.fold_in(key, salt), (NF, NH, NW, INNER), jnp.float32)
    return jnp.clip(base, -6.0, 6.0)


def draw_queries(key, part):
    field = lifted_field(key, 11)
    return jnp.clip(field, -250.0, 250.0).astype(jnp.bfloat16)


def draw_keys(key, part):
    field = lifted_field(key, 21)
    return jnp.clip(field, -250.0, 250.0).astype(jnp.bfloat16)


def plant(result, own_key, least, largest):
    longest = result.shape.index(max(result.shape))
    spots = []
    for shift in (0, 1):
        where = [jax.random.randint(jax.random.fold_in(own_key, axis), (), 0, length) for axis, length in enumerate(result.shape)]
        where[longest] = (where[longest] + shift) % result.shape[longest]
        spots.append(tuple(where))
    return result.at[spots[0]].set(least).at[spots[1]].set(largest)


def shard_levels(rng, shape, shards, low, top_value):
    loudness = 1.0
    for position, shards_of in shards:
        steps = jax.random.uniform(jax.random.fold_in(jax.random.fold_in(rng, 6), position), (shards_of,), jnp.float32, low / len(shards), top_value / len(shards))
        loudness = loudness * jnp.repeat(jnp.exp(steps), shape[position] // shards_of).reshape((-1,) + (1,) * (len(shape) - 1 - position))
    return loudness


def gaussian(rng, shape, scale, limit, split=(), held_as=jnp.bfloat16):
    result = scale * jax.random.normal(rng, shape, jnp.float32)
    if split:
        result = result * shard_levels(rng, shape, split, -0.22, 0.18)
    return jnp.clip(result, -limit, limit).astype(held_as)


def setup_inputs(seed: int = 0) -> dict:
    key_list = jax.random.split(jax.random.key(seed), 12)
    hidden_in = gaussian(key_list[0], (NF, NH, NW, D), 1.0, 6.0, ((0, 8), (1, 32)))
    queries = draw_queries(jax.random.fold_in(key_list[11], 71), 0)
    keys = draw_keys(jax.random.fold_in(key_list[11], 71), 0)
    values = gaussian(key_list[3], (NF, NH, NW, INNER), 1.0, 6.0, ((0, 8), (1, 32)))
    query_gain = jnp.clip(jnp.exp(jax.random.uniform(key_list[4], (INNER,), jnp.float32, math.log(0.5), math.log(3.0))), 0.5, 3.0)
    key_gain = jnp.clip(jnp.exp(jax.random.uniform(key_list[5], (INNER,), jnp.float32, math.log(0.5), math.log(3.0))), 0.5, 3.0)
    reach_time = plant(jax.random.randint(key_list[6], (HEADS,), 0, 2), jax.random.fold_in(key_list[6], 1), 0, 1).astype(jnp.int32)
    reach_rows = plant(jax.random.randint(key_list[7], (HEADS,), 0, 2), jax.random.fold_in(key_list[7], 1), 0, 1).astype(jnp.int32)
    reach_cols = plant(jax.random.randint(key_list[8], (HEADS,), 0, 3), jax.random.fold_in(key_list[8], 1), 0, 2).astype(jnp.int32)
    out_weight = gaussian(key_list[9], (INNER, D), (INNER // 8) ** -0.5, 0.25, ((0, 32), (1, 8)))
    gate = jnp.clip(jax.random.uniform(key_list[10], (D,), jnp.float32, -1.5, 1.5), -1.5, 1.5)
    return dict(hidden_in=hidden_in, queries=queries, keys=keys, values=values, query_gain=query_gain, key_gain=key_gain, reach_time=reach_time, reach_rows=reach_rows, reach_cols=reach_cols, out_weight=out_weight, gate=gate)


def normalize(source, gain):
    values_f = source.astype(jnp.float32)
    mean_square = lax.optimization_barrier(jnp.mean(values_f * values_f, axis=-1, keepdims=True))
    return (values_f * lax.rsqrt(mean_square + 1e-06) * gain).astype(jnp.bfloat16)

def attend(query_block, key_region, value_region, first_frame, first_row, frame_count, row_count, reach_time, reach_rows, reach_cols):
    frames_here, rows_here, columns, inner = query_block.shape
    head_count = reach_time.shape[0]
    head_width = inner // head_count
    query_flat = query_block.reshape(-1, head_count, head_width).astype(jnp.float32)
    key_flat = key_region.reshape(-1, head_count, head_width).astype(jnp.float32)
    value_flat = value_region.reshape(-1, head_count, head_width).astype(jnp.float32)
    frame_q = first_frame + jnp.arange(frames_here, dtype=jnp.int32)
    frame_k = first_frame - 1 + jnp.arange(frames_here + 2, dtype=jnp.int32)
    row_q = first_row + jnp.arange(rows_here, dtype=jnp.int32)
    row_k = first_row - 1 + jnp.arange(rows_here + 2, dtype=jnp.int32)
    tiles = jnp.arange(columns, dtype=jnp.int32) // TW
    query_shape = (frames_here, rows_here, columns)
    key_shape = (frames_here + 2, rows_here + 2, columns)
    query_frame = jnp.broadcast_to(frame_q[:, None, None], query_shape).reshape(-1)
    query_row = jnp.broadcast_to(row_q[None, :, None], query_shape).reshape(-1)
    query_tile = jnp.broadcast_to(tiles[None, None, :], query_shape).reshape(-1)
    key_frame = jnp.broadcast_to(frame_k[:, None, None], key_shape).reshape(-1)
    key_row = jnp.broadcast_to(row_k[None, :, None], key_shape).reshape(-1)
    key_tile = jnp.broadcast_to(tiles[None, None, :], key_shape).reshape(-1)
    frame_gap = jnp.abs(query_frame[:, None] - key_frame[None, :])
    row_gap = jnp.abs(query_row[:, None] - key_row[None, :])
    tile_gap = jnp.abs(query_tile[:, None] - key_tile[None, :])
    inside = (key_frame >= 0) & (key_frame < frame_count) & (key_row >= 0) & (key_row < row_count)
    allowed = (frame_gap[None] <= reach_time[:, None, None]) & (row_gap[None] <= reach_rows[:, None, None])
    allowed = allowed & (tile_gap[None] <= reach_cols[:, None, None]) & inside[None, None, :]
    scores = jnp.einsum('qhd,khd->hqk', query_flat, key_flat) * head_width ** (-0.5)
    masked = jnp.where(allowed, scores, -jnp.inf)
    row_peak = lax.optimization_barrier(jnp.max(masked, axis=2, keepdims=True))
    weights = jnp.exp(masked - row_peak)
    totals = lax.optimization_barrier(jnp.sum(weights, axis=2, keepdims=True))
    rounded = weights.astype(jnp.bfloat16)
    mixed = jnp.einsum('hqk,khd->qhd', rounded.astype(jnp.float32), value_flat)
    mixed = mixed / jnp.transpose(totals, (1, 0, 2))
    return mixed.reshape(mixed.shape[0], inner).astype(jnp.bfloat16)

def reference(hidden_in, queries, keys, values, query_gain, key_gain, reach_time, reach_rows, reach_cols, out_weight, gate):
    query_norm = normalize(queries, query_gain)
    key_norm = normalize(keys, key_gain)
    padding = ((1, 1), (1, 1), (0, 0), (0, 0))
    key_pad = jnp.pad(key_norm, padding)
    value_pad = jnp.pad(values, padding)
    row_blocks = NH // RH
    block_count = NF // FR * row_blocks

    def one_block(block_index):
        first_frame = (block_index // row_blocks * FR).astype(jnp.int32)
        first_row = (block_index % row_blocks * RH).astype(jnp.int32)
        anchor = jnp.zeros((), jnp.int32)
        query_block = lax.dynamic_slice(query_norm, (first_frame, first_row, anchor, anchor), (FR, RH, NW, INNER))
        key_region = lax.dynamic_slice(key_pad, (first_frame, first_row, anchor, anchor), (FR + 2, RH + 2, NW, INNER))
        value_region = lax.dynamic_slice(value_pad, (first_frame, first_row, anchor, anchor), (FR + 2, RH + 2, NW, INNER))
        attention = attend(query_block, key_region, value_region, first_frame, first_row, NF, NH, reach_time, reach_rows, reach_cols)
        hidden_block = lax.dynamic_slice(hidden_in, (first_frame, first_row, anchor, anchor), (FR, RH, NW, D))
        hidden_flat = hidden_block.reshape(-1, D).astype(jnp.float32)
        branch = jnp.dot(attention, out_weight, preferred_element_type=jnp.float32)
        return (hidden_flat + gate * branch).astype(jnp.bfloat16).reshape(FR, RH, NW, D)
    blocks = lax.map(one_block, jnp.arange(block_count, dtype=jnp.int32))
    blocks = blocks.reshape(NF // FR, NH // RH, FR, RH, NW, D)
    return jnp.transpose(blocks, (0, 2, 1, 3, 4, 5)).reshape(NF, NH, NW, D)
```

```python
import functools

import jax
import jax.numpy as jnp
from jax import lax
from jax.experimental import pallas as pl
from jax.experimental.pallas import tpu as pltpu
from jax.sharding import Mesh, PartitionSpec as P

TW = 8
HEAD = 128
TM = ("y_lo", "x")
SP = ("y_hi", "z", "core")
CHUNKS = 1
COMBOS = 12
F32, BF16 = jnp.float32, jnp.bfloat16


def axis_size(axes):
    n = 1
    for a in axes:
        n *= lax.axis_size(a)
    return n


def passed_along(block, axes, distance):
    n = axis_size(axes)
    route = [(i - distance, i) for i in range(n) if 0 <= i - distance < n]
    return lax.ppermute(block, axes, route)


def shifted(block, axis, distance):
    n = lax.axis_size(axis)
    return lax.ppermute(block, axis, [(i, (i + distance) % n) for i in range(n)])


def params(megabytes=48):
    return pltpu.CompilerParams(vmem_limit_bytes=megabytes << 20)


def prepare_kernel(q_ref, k_ref, v_ref, qg_ref, kg_ref, qn_ref, *outs):
    i = pl.program_id(0)
    f, r = i // 2, i % 2
    inner = q_ref.shape[-1]

    def normed(ref, gain):
        a = ref[0].astype(F32)
        ms = jnp.sum(a * a, axis=-1, keepdims=True) * (1.0 / inner)
        return (a * lax.rsqrt(ms + 1e-06) * gain[...]).astype(BF16)

    qn_ref[0] = normed(q_ref, qg_ref)
    kn = normed(k_ref, kg_ref)
    v = v_ref[0]
    width = inner // (len(outs) // 4)
    for c in range(len(outs) // 4):
        f0, f1, r0, r1 = outs[4 * c : 4 * c + 4]
        lanes = slice(c * width, (c + 1) * width)
        for which, ref in ((0, f0), (1, f1)):

            @pl.when(f == which)
            def _(ref=ref):
                ref[0, 0] = kn[:, lanes]
                ref[1, 0] = v[:, lanes]

        for which, ref in ((0, r0), (1, r1)):

            @pl.when(r == which)
            def _(ref=ref):
                ref[0, 0] = kn[:, lanes]
                ref[0, 1] = v[:, lanes]


def prepare(queries, keys, values, query_gain, key_gain):
    groups, nw, inner = queries.shape
    width = inner // CHUNKS
    token_spec = pl.BlockSpec((1, nw, inner), lambda i: (i, 0, 0))
    gain_spec = pl.BlockSpec((1, inner), lambda i: (0, 0))
    out_shape = [jax.ShapeDtypeStruct(queries.shape, BF16)]
    out_specs = [token_spec]
    for _ in range(CHUNKS):
        out_shape += [jax.ShapeDtypeStruct((2, 2, nw, width), BF16)] * 4
        out_specs += [
            pl.BlockSpec((2, 1, nw, width), lambda i: (0, jnp.minimum(i, 1), 0, 0)),
            pl.BlockSpec((2, 1, nw, width), lambda i: (0, jnp.maximum(i - 2, 0), 0, 0)),
            pl.BlockSpec((1, 2, nw, width), lambda i: (i // 2, 0, 0, 0)),
            pl.BlockSpec((1, 2, nw, width), lambda i: (i // 2, 0, 0, 0)),
        ]
    return pl.pallas_call(
        prepare_kernel,
        grid=(groups,),
        in_specs=[token_spec] * 3 + [gain_spec] * 2,
        out_specs=out_specs,
        out_shape=out_shape,
        compiler_params=params(),
        cost_estimate=pl.CostEstimate(flops=0, bytes_accessed=12 << 20, transcendentals=0),
        name="prepare",
    )(queries, keys, values, query_gain[None], key_gain[None])


def mask_tables(first_frame, first_row, frame_count, row_count, nw):
    i32 = jnp.int32
    shape = (COMBOS, 2, 2 * nw, 3 * 4 * nw)
    t = lax.broadcasted_iota(i32, shape, 0)
    f = lax.broadcasted_iota(i32, shape, 1)
    q = lax.broadcasted_iota(i32, shape, 2)
    k = lax.broadcasted_iota(i32, shape, 3)
    kf, kr, kc = k // (4 * nw), k // nw % 4, k % nw
    frame, row = first_frame - 1 + f + kf, first_row - 1 + kr
    allowed = jnp.abs(kf - 1) <= t // 6
    allowed &= jnp.abs(q // nw + 1 - kr) <= t // 3 % 2
    allowed &= jnp.abs(q % nw // TW - kc // TW) <= t % 3
    allowed &= (frame >= 0) & (frame < frame_count) & (row >= 0) & (row < row_count)
    return jnp.where(allowed, 0.0, -jnp.inf).astype(F32)


def attend_kernel(heads, scale, combo_ref, q_ref, f0, f1, hb, ha, rb, ra, cb, ca, mask_ref, out_ref):
    step = pl.program_id(0)
    for h in range(heads):
        lanes = slice(h * HEAD, (h + 1) * HEAD)
        combo = combo_ref[step * heads + h]

        def region(kv):
            frames = ((cb[0], hb, ca[0]), (rb[0], f0, ra[0]), (rb[1], f1, ra[1]), (cb[1], ha, ca[1]))
            parts = []
            for below, own, above in frames:
                parts += [below[kv, :, lanes], own[kv, 0, :, lanes], own[kv, 1, :, lanes], above[kv, :, lanes]]
            return jnp.concatenate(parts, axis=0)

        keys, values = region(0), region(1)
        span = keys.shape[0] // 4 * 3
        for f in range(2):
            first = f * (span // 3)
            q = q_ref[2 * f : 2 * f + 2, :, lanes].reshape(-1, HEAD)
            s = lax.dot_general(
                q, keys[first : first + span], (((1,), (1,)), ((), ())), preferred_element_type=F32
            )
            s = s + mask_ref[combo, f]
            peak = jnp.max(s, axis=1, keepdims=True)
            w = jnp.exp((s - peak) * scale)
            total = jnp.sum(w, axis=1, keepdims=True)
            o = jnp.dot(w.astype(BF16), values[first : first + span], preferred_element_type=F32)
            out_ref[2 * f : 2 * f + 2, :, lanes] = (o / total).astype(BF16).reshape(2, -1, HEAD)


def attend(combo, chunk, qn, own, halos, masks, heads=4):
    groups, nw, inner = qn.shape
    width = own[0].shape[-1]
    lanes = heads * HEAD
    steps = width // lanes
    kv_spec = pl.BlockSpec((2, 2, nw, lanes), lambda i, *_: (0, 0, 0, i))
    return pl.pallas_call(
        functools.partial(attend_kernel, heads, HEAD**-0.5),
        grid_spec=pltpu.PrefetchScalarGridSpec(
            num_scalar_prefetch=1,
            grid=(steps,),
            in_specs=[pl.BlockSpec((groups, nw, lanes), lambda i, *_: (0, 0, chunk * steps + i))]
            + [kv_spec] * 8
            + [pl.BlockSpec(masks.shape, lambda i, *_: (0, 0, 0, 0))],
            out_specs=pl.BlockSpec((groups, nw, lanes), lambda i, *_: (0, 0, i)),
        ),
        out_shape=jax.ShapeDtypeStruct((groups, nw, width), BF16),
        compiler_params=params(),
        cost_estimate=pl.CostEstimate(flops=4 * 128 * 384 * width, bytes_accessed=32 << 20, transcendentals=0),
        name="attend",
    )(combo, qn, *own, *halos, masks)


def project_kernel(a0, a1, a2, a3, w_ref, o0, o1, o2, o3, acc):
    k = pl.program_id(0)
    a = jnp.concatenate([a0[...], a1[...], a2[...], a3[...]], axis=0)
    half = w_ref.shape[-1]
    for n in range(2):
        cols = slice(n * half, (n + 1) * half)
        term = jnp.dot(a, w_ref[n], preferred_element_type=F32)

        @pl.when(k == 0)
        def _():
            acc[:, cols] = term

        @pl.when(k > 0)
        def _():
            acc[:, cols] += term

    @pl.when(k == pl.num_programs(0) - 1)
    def _():
        rows = a0.shape[0]
        for d, o in enumerate((o0, o1, o2, o3)):
            o[...] = acc[d * rows : (d + 1) * rows, :].astype(BF16)


def project(blocks, weight, step=1024):
    rows, inner = blocks[0].shape
    cols = 2 * weight.shape[-1]
    return pl.pallas_call(
        project_kernel,
        grid=(inner // step,),
        in_specs=[pl.BlockSpec((rows, step), lambda k: (0, k))] * 4
        + [pl.BlockSpec((2, step, cols // 2), lambda k: (0, k, 0))],
        out_specs=[pl.BlockSpec((rows, cols), lambda k: (0, 0))] * 4,
        out_shape=[jax.ShapeDtypeStruct((rows, cols), BF16)] * 4,
        scratch_shapes=[pltpu.VMEM((4 * rows, cols), F32)],
        compiler_params=params(),
        cost_estimate=pl.CostEstimate(flops=8 * rows * inner * cols, bytes_accessed=20 << 20, transcendentals=0),
        name="project",
    )(*blocks, weight)


def finish_kernel(x_ref, hidden, gate, p0, p1, p2, p3, out):
    cols = p0.shape[-1] // 2
    for d, p in enumerate((p0, p1, p2, p3)):
        x = lax.rem(x_ref[0] + d, 4)
        for n in range(2):
            where = pl.ds(pl.multiple_of((n * 4 + x) * cols, HEAD), cols)
            term = gate[:, where] * p[:, n * cols : (n + 1) * cols].astype(F32)
            out[:, where] = (hidden[:, where].astype(F32) + term).astype(BF16)


def finish(x, hidden, gate, pieces, blocks=4):
    rows, width = hidden.shape
    step = rows // blocks
    row_spec = pl.BlockSpec((step, width), lambda i, *_: (i, 0))
    return pl.pallas_call(
        finish_kernel,
        grid_spec=pltpu.PrefetchScalarGridSpec(
            num_scalar_prefetch=1,
            grid=(blocks,),
            in_specs=[row_spec, pl.BlockSpec((1, width), lambda i, *_: (0, 0))]
            + [pl.BlockSpec((step, pieces[0].shape[1]), lambda i, *_: (i, 0))] * 4,
            out_specs=row_spec,
        ),
        out_shape=jax.ShapeDtypeStruct(hidden.shape, BF16),
        compiler_params=params(),
        name="finish",
    )(x, hidden, gate[None], *pieces)


def shards(hidden_in, queries, keys, values, query_gain, key_gain, reach_time, reach_rows, reach_cols, out_weight, gate):
    frames, rows, nw, inner = queries.shape
    width = hidden_in.shape[3]
    weight = lax.all_gather(out_weight, ("y_lo",) + SP, axis=0, tiled=True)
    weight = weight.reshape(2, inner, out_weight.shape[1])

    tokens = [a.reshape(frames * rows, nw, inner) for a in (queries, keys, values)]
    qn, *own = prepare(*tokens, query_gain, key_gain)
    masks = mask_tables(
        lax.axis_index(TM) * frames,
        lax.axis_index(SP) * rows,
        frames * axis_size(TM),
        rows * axis_size(SP),
        nw,
    )
    combo = reach_time * 6 + reach_rows * 3 + reach_cols
    heads = reach_time.shape[0] // CHUNKS
    outs = []
    for c in range(CHUNKS):
        f0, f1, r0, r1 = own[4 * c : 4 * c + 4]
        hb, ha = passed_along(f1, TM, 1), passed_along(f0, TM, -1)
        rb, ra = passed_along(r1, SP, 1), passed_along(r0, SP, -1)
        cb = passed_along(jnp.stack([hb[:, 1], ha[:, 1]]), SP, 1)
        ca = passed_along(jnp.stack([hb[:, 0], ha[:, 0]]), SP, -1)
        a = attend(combo[c * heads : (c + 1) * heads], c, qn, (f0, f1), (hb, ha, rb, ra, cb, ca), masks)
        outs.append(a.reshape(frames * rows * nw, inner // CHUNKS))
    a = outs[0]
    blocks = [a] + [shifted(a, "x", d) for d in (1, 2, 3)]
    terms = project(blocks, weight)
    pieces = [terms[0]] + [shifted(terms[d], "x", -d) for d in (1, 2, 3)]
    x = lax.axis_index("x").astype(jnp.int32)[None]
    out = finish(x, hidden_in.reshape(-1, width), gate, pieces)
    return out.reshape(hidden_in.shape)


def solution(mesh):
    inner_mesh = Mesh(mesh.devices.reshape(2, 4, 2, 8, 2), TM + SP)
    tokens = P(TM, SP, None, None)
    in_specs = (tokens,) * 4 + (P(),) * 5 + (P(SP, TM), P())
    return jax.shard_map(shards, mesh=inner_mesh, in_specs=in_specs, out_specs=tokens, check_vma=False)
```

```python
import functools

import jax
import jax.numpy as jnp
from jax import lax
from jax.experimental import pallas as pl
from jax.experimental.pallas import tpu as pltpu
from jax.sharding import Mesh, PartitionSpec as P

TW = 8
HEAD = 128
TM = ("y_lo", "x")
SP = ("y_hi", "z", "core")
CHUNKS = 1
COMBOS = 12
F32, BF16 = jnp.float32, jnp.bfloat16


def axis_size(axes):
    n = 1
    for a in axes:
        n *= lax.axis_size(a)
    return n


def passed_along(block, axes, distance):
    n = axis_size(axes)
    route = [(i - distance, i) for i in range(n) if 0 <= i - distance < n]
    return lax.ppermute(block, axes, route)


def shifted(block, axis, distance):
    n = lax.axis_size(axis)
    return lax.ppermute(block, axis, [(i, (i + distance) % n) for i in range(n)])


def params(megabytes=24):
    return pltpu.CompilerParams(vmem_limit_bytes=megabytes << 20)


def prepare_kernel(q_ref, k_ref, v_ref, qg_ref, kg_ref, qn_ref, *outs):
    i = pl.program_id(0)
    f, r = i // 2, i % 2
    inner = q_ref.shape[-1]

    def normed(ref, gain):
        a = ref[0].astype(F32)
        ms = jnp.sum(a * a, axis=-1, keepdims=True) * (1.0 / inner)
        return (a * lax.rsqrt(ms + 1e-06) * gain[...]).astype(BF16)

    qn_ref[0] = normed(q_ref, qg_ref)
    kn = normed(k_ref, kg_ref)
    v = v_ref[0]
    width = inner // (len(outs) // 4)
    for c in range(len(outs) // 4):
        f0, f1, r0, r1 = outs[4 * c : 4 * c + 4]
        lanes = slice(c * width, (c + 1) * width)
        for which, ref in ((0, f0), (1, f1)):

            @pl.when(f == which)
            def _(ref=ref):
                ref[0, 0] = kn[:, lanes]
                ref[0, 1] = v[:, lanes]

        for which, ref in ((0, r0), (1, r1)):

            @pl.when(r == which)
            def _(ref=ref):
                ref[0, 0] = kn[:, lanes]
                ref[0, 1] = v[:, lanes]


def prepare(queries, keys, values, query_gain, key_gain):
    groups, nw, inner = queries.shape
    width = inner // CHUNKS
    token_spec = pl.BlockSpec((1, nw, inner), lambda i: (i, 0, 0))
    gain_spec = pl.BlockSpec((1, inner), lambda i: (0, 0))
    out_shape = [jax.ShapeDtypeStruct(queries.shape, BF16)]
    out_specs = [token_spec]
    for _ in range(CHUNKS):
        out_shape += [jax.ShapeDtypeStruct((2, 2, nw, width), BF16)] * 4
        out_specs += [
            pl.BlockSpec((1, 2, nw, width), lambda i: (jnp.minimum(i, 1), 0, 0, 0)),
            pl.BlockSpec((1, 2, nw, width), lambda i: (jnp.maximum(i - 2, 0), 0, 0, 0)),
            pl.BlockSpec((1, 2, nw, width), lambda i: (i // 2, 0, 0, 0)),
            pl.BlockSpec((1, 2, nw, width), lambda i: (i // 2, 0, 0, 0)),
        ]
    return pl.pallas_call(
        prepare_kernel,
        grid=(groups,),
        in_specs=[token_spec] * 3 + [gain_spec] * 2,
        out_specs=out_specs,
        out_shape=out_shape,
        compiler_params=params(),
        cost_estimate=pl.CostEstimate(flops=0, bytes_accessed=12 << 20, transcendentals=0),
        name="prepare",
    )(queries, keys, values, query_gain[None], key_gain[None])


def mask_tables(first_frame, first_row, frame_count, row_count, nw):
    i32 = jnp.int32
    shape = (COMBOS, 2, 2 * nw, 3 * 4 * nw)
    t = lax.broadcasted_iota(i32, shape, 0)
    f = lax.broadcasted_iota(i32, shape, 1)
    q = lax.broadcasted_iota(i32, shape, 2)
    k = lax.broadcasted_iota(i32, shape, 3)
    kf, kr, kc = k // (4 * nw), k // nw % 4, k % nw
    frame, row = first_frame - 1 + f + kf, first_row - 1 + kr
    allowed = jnp.abs(kf - 1) <= t // 6
    allowed &= jnp.abs(q // nw + 1 - kr) <= t // 3 % 2
    allowed &= jnp.abs(q % nw // TW - kc // TW) <= t % 3
    allowed &= (frame >= 0) & (frame < frame_count) & (row >= 0) & (row < row_count)
    return jnp.where(allowed, 0.0, -jnp.inf).astype(F32)


def attend_kernel(heads, scale, combo_ref, q_ref, f0, f1, hb, ha, rb, ra, cb, ca, mask_ref, *out_refs):
    step = pl.program_id(0)
    for h in range(heads):
        lanes = slice(h * HEAD, (h + 1) * HEAD)
        combo = combo_ref[step * heads + h]

        def region(kv):
            frames = ((cb[0], hb, ca[0]), (rb[0], f0, ra[0]), (rb[1], f1, ra[1]), (cb[1], ha, ca[1]))
            parts = []
            for below, own, above in frames:
                parts += [below[kv, :, lanes], own[0, kv, :, lanes], own[1, kv, :, lanes], above[kv, :, lanes]]
            return jnp.concatenate(parts, axis=0)

        keys, values = region(0), region(1)
        span = keys.shape[0] // 4 * 3
        for f in range(2):
            first = f * (span // 3)
            q = q_ref[2 * f : 2 * f + 2, :, lanes].reshape(-1, HEAD)
            s = lax.dot_general(
                q, keys[first : first + span], (((1,), (1,)), ((), ())), preferred_element_type=F32
            )
            s = s + mask_ref[combo, f]
            peak = jnp.max(s, axis=1, keepdims=True)
            w = jnp.exp((s - peak) * scale)
            total = jnp.sum(w, axis=1, keepdims=True)
            o = jnp.dot(w.astype(BF16), values[first : first + span], preferred_element_type=F32)
            out_refs[f][:, lanes] = (o / total).astype(BF16)


def attend(combo, chunk, qn, own, halos, masks, heads=4):
    groups, nw, inner = qn.shape
    width = own[0].shape[-1]
    lanes = heads * HEAD
    steps = width // lanes
    kv_spec = pl.BlockSpec((2, 2, nw, lanes), lambda i, *_: (0, 0, 0, i))
    return pl.pallas_call(
        functools.partial(attend_kernel, heads, HEAD**-0.5),
        grid_spec=pltpu.PrefetchScalarGridSpec(
            num_scalar_prefetch=1,
            grid=(steps,),
            in_specs=[pl.BlockSpec((groups, nw, lanes), lambda i, *_: (0, 0, chunk * steps + i))]
            + [kv_spec] * 8
            + [pl.BlockSpec(masks.shape, lambda i, *_: (0, 0, 0, 0))],
            out_specs=[pl.BlockSpec((2 * nw, lanes), lambda i, *_: (0, i))] * 2,
        ),
        out_shape=[jax.ShapeDtypeStruct((2 * nw, width), BF16)] * 2,
        compiler_params=params(),
        cost_estimate=pl.CostEstimate(flops=4 * 128 * 384 * width, bytes_accessed=32 << 20, transcendentals=0),
        name="attend",
    )(combo, qn, *own, *halos, masks)


def project_kernel(blocks, *refs):
    ins, w_ref, outs, acc = refs[:blocks], refs[blocks], refs[blocks + 1 : -1], refs[-1]
    k = pl.program_id(0)
    a = jnp.concatenate([i[...] for i in ins], axis=0)
    half = w_ref.shape[-1]
    for n in range(2):
        cols = slice(n * half, (n + 1) * half)
        term = jnp.dot(a, w_ref[0, n], preferred_element_type=F32)

        @pl.when(k == 0)
        def _():
            acc[:, cols] = term

        @pl.when(k > 0)
        def _():
            acc[:, cols] += term

    @pl.when(k == pl.num_programs(0) - 1)
    def _():
        rows = outs[0].shape[0]
        for d, o in enumerate(outs):
            o[...] = acc[d * rows : (d + 1) * rows, :].astype(BF16)


def project(blocks, weight, step=1280):
    rows, inner = blocks[0].shape
    groups, halves, depth, half = weight.shape
    cols, devices, inside = halves * half, len(blocks) // 2, depth // step
    return pl.pallas_call(
        functools.partial(project_kernel, len(blocks)),
        grid=(groups * inside,),
        in_specs=[pl.BlockSpec((rows, step), lambda k: (0, k))] * len(blocks)
        + [pl.BlockSpec((1, halves, step, half), lambda k: (k // inside, 0, k % inside, 0))],
        out_specs=[pl.BlockSpec((2 * rows, cols), lambda k: (0, 0))] * devices,
        out_shape=[jax.ShapeDtypeStruct((2 * rows, cols), BF16)] * devices,
        scratch_shapes=[pltpu.VMEM((2 * devices * rows, cols), F32)],
        compiler_params=params(),
        cost_estimate=pl.CostEstimate(
            flops=4 * devices * rows * inner * cols, bytes_accessed=2 * inner * cols, transcendentals=0
        ),
        name="project",
    )(*blocks, weight)


def finish_kernel(x_ref, hidden, gate, p0, p1, p2, p3, out):
    cols = p0.shape[-1] // 2
    for d, p in enumerate((p0, p1, p2, p3)):
        x = lax.rem(x_ref[0] + d, 4)
        for n in range(2):
            where = pl.ds(pl.multiple_of((n * 4 + x) * cols, HEAD), cols)
            term = gate[:, where] * p[:, n * cols : (n + 1) * cols].astype(F32)
            out[:, where] = (hidden[:, where].astype(F32) + term).astype(BF16)


def finish(x, hidden, gate, pieces, blocks=4):
    rows, width = hidden.shape
    step = rows // blocks
    row_spec = pl.BlockSpec((step, width), lambda i, *_: (i, 0))
    return pl.pallas_call(
        finish_kernel,
        grid_spec=pltpu.PrefetchScalarGridSpec(
            num_scalar_prefetch=1,
            grid=(blocks,),
            in_specs=[row_spec, pl.BlockSpec((1, width), lambda i, *_: (0, 0))]
            + [pl.BlockSpec((step, pieces[0].shape[1]), lambda i, *_: (i, 0))] * 4,
            out_specs=row_spec,
        ),
        out_shape=jax.ShapeDtypeStruct(hidden.shape, BF16),
        compiler_params=params(),
        name="finish",
    )(x, hidden, gate[None], *pieces)


def shards(hidden_in, queries, keys, values, query_gain, key_gain, reach_time, reach_rows, reach_cols, out_weight, gate):
    frames, rows, nw, inner = queries.shape
    width = hidden_in.shape[3]
    weight = lax.all_gather(out_weight, ("y_hi", "y_lo", "z", "core"), axis=0, tiled=True)
    weight = weight.reshape(2, 2, inner // 2, out_weight.shape[1])

    tokens = [a.reshape(frames * rows, nw, inner) for a in (queries, keys, values)]
    qn, *own = prepare(*tokens, query_gain, key_gain)
    masks = mask_tables(
        lax.axis_index(TM) * frames,
        lax.axis_index(SP) * rows,
        frames * axis_size(TM),
        rows * axis_size(SP),
        nw,
    )
    combo = reach_time * 6 + reach_rows * 3 + reach_cols
    heads = reach_time.shape[0] // CHUNKS
    outs = []
    for c in range(CHUNKS):
        f0, f1, r0, r1 = own[4 * c : 4 * c + 4]
        hb, ha = passed_along(f1, TM, 1), passed_along(f0, TM, -1)
        rb, ra = passed_along(r1, SP, 1), passed_along(r0, SP, -1)
        cb = passed_along(jnp.stack([hb[1], ha[1]]), SP, 1)
        ca = passed_along(jnp.stack([hb[0], ha[0]]), SP, -1)
        a = attend(combo[c * heads : (c + 1) * heads], c, qn, (f0, f1), (hb, ha, rb, ra, cb, ca), masks)
        outs.append(a)
    a0, a1 = outs[0]
    left0, right1 = shifted(a0, "x", 1), shifted(a1, "x", -1)
    left1, right0 = shifted(a1, "x", 1), shifted(a0, "x", -1)
    far0, far1 = shifted(left0, "x", 1), shifted(right1, "x", -1)
    mine, near_left, near_right = project([a0, a1, left0, left1, right0, right1], weight)
    (far,) = project([far0, far1], weight)
    pieces = [mine, shifted(near_left, "x", -1), shifted(far, "x", 2), shifted(near_right, "x", 1)]
    x = lax.axis_index("x").astype(jnp.int32)[None]
    out = finish(x, hidden_in.reshape(-1, width), gate, pieces)
    return out.reshape(hidden_in.shape)


def solution(mesh):
    inner_mesh = Mesh(mesh.devices.reshape(2, 4, 2, 8, 2), TM + SP)
    tokens = P(TM, SP, None, None)
    in_specs = (tokens,) * 4 + (P(),) * 5 + (P(SP, TM), P())
    return jax.shard_map(shards, mesh=inner_mesh, in_specs=in_specs, out_specs=tokens, check_vma=False)
```

```python
import functools

import jax
import jax.numpy as jnp
from jax import lax
from jax.experimental import pallas as pl
from jax.experimental.pallas import tpu as pltpu
from jax.sharding import Mesh, PartitionSpec as P

TW = 8
HEAD = 128
TM = ("y_lo", "x")
SP = ("y_hi", "z", "core")
CHUNKS = 1
COMBOS = 12
F32, BF16 = jnp.float32, jnp.bfloat16


def axis_size(axes):
    n = 1
    for a in axes:
        n *= lax.axis_size(a)
    return n


def passed_along(block, axes, distance):
    n = axis_size(axes)
    route = [(i - distance, i) for i in range(n) if 0 <= i - distance < n]
    return lax.ppermute(block, axes, route)


def shifted(block, axis, distance):
    n = lax.axis_size(axis)
    return lax.ppermute(block, axis, [(i, (i + distance) % n) for i in range(n)])


def in_hbm(array):
    return pltpu.with_memory_space_constraint(array, pltpu.HBM)


def params(megabytes=24):
    return pltpu.CompilerParams(vmem_limit_bytes=megabytes << 20)


def prepare_kernel(q_ref, k_ref, v_ref, qg_ref, kg_ref, qn_ref, *outs):
    i = pl.program_id(0)
    f, r = i // 2, i % 2
    inner = q_ref.shape[-1]

    def normed(ref, gain):
        a = ref[0].astype(F32)
        ms = jnp.sum(a * a, axis=-1, keepdims=True) * (1.0 / inner)
        return (a * lax.rsqrt(ms + 1e-06) * gain[...]).astype(BF16)

    qn_ref[0] = normed(q_ref, qg_ref)
    kn = normed(k_ref, kg_ref)
    v = v_ref[0]
    width = inner // (len(outs) // 4)
    for c in range(len(outs) // 4):
        f0, f1, r0, r1 = outs[4 * c : 4 * c + 4]
        lanes = slice(c * width, (c + 1) * width)
        for which, ref in ((0, f0), (1, f1)):

            @pl.when(f == which)
            def _(ref=ref):
                ref[0, 0] = kn[:, lanes]
                ref[0, 1] = v[:, lanes]

        for which, ref in ((0, r0), (1, r1)):

            @pl.when(r == which)
            def _(ref=ref):
                ref[0, 0] = kn[:, lanes]
                ref[0, 1] = v[:, lanes]


def prepare(queries, keys, values, query_gain, key_gain):
    groups, nw, inner = queries.shape
    width = inner // CHUNKS
    token_spec = pl.BlockSpec((1, nw, inner), lambda i: (i, 0, 0))
    gain_spec = pl.BlockSpec((1, inner), lambda i: (0, 0))
    out_shape = [jax.ShapeDtypeStruct(queries.shape, BF16)]
    out_specs = [token_spec]
    for _ in range(CHUNKS):
        out_shape += [jax.ShapeDtypeStruct((2, 2, nw, width), BF16)] * 4
        out_specs += [
            pl.BlockSpec((1, 2, nw, width), lambda i: (jnp.minimum(i, 1), 0, 0, 0)),
            pl.BlockSpec((1, 2, nw, width), lambda i: (jnp.maximum(i - 2, 0), 0, 0, 0)),
            pl.BlockSpec((1, 2, nw, width), lambda i: (i // 2, 0, 0, 0)),
            pl.BlockSpec((1, 2, nw, width), lambda i: (i // 2, 0, 0, 0)),
        ]
    return pl.pallas_call(
        prepare_kernel,
        grid=(groups,),
        in_specs=[token_spec] * 3 + [gain_spec] * 2,
        out_specs=out_specs,
        out_shape=out_shape,
        compiler_params=params(),
        cost_estimate=pl.CostEstimate(flops=0, bytes_accessed=12 << 20, transcendentals=0),
        name="prepare",
    )(*[in_hbm(a) for a in (queries, keys, values)], query_gain[None], key_gain[None])


def mask_tables(first_frame, first_row, frame_count, row_count, nw):
    i32 = jnp.int32
    shape = (COMBOS, 2, 2 * nw, 3 * 4 * nw)
    t = lax.broadcasted_iota(i32, shape, 0)
    f = lax.broadcasted_iota(i32, shape, 1)
    q = lax.broadcasted_iota(i32, shape, 2)
    k = lax.broadcasted_iota(i32, shape, 3)
    kf, kr, kc = k // (4 * nw), k // nw % 4, k % nw
    frame, row = first_frame - 1 + f + kf, first_row - 1 + kr
    allowed = jnp.abs(kf - 1) <= t // 6
    allowed &= jnp.abs(q // nw + 1 - kr) <= t // 3 % 2
    allowed &= jnp.abs(q % nw // TW - kc // TW) <= t % 3
    allowed &= (frame >= 0) & (frame < frame_count) & (row >= 0) & (row < row_count)
    return jnp.where(allowed, 0.0, -jnp.inf).astype(F32)


def attend_kernel(heads, scale, combo_ref, q_ref, f0, f1, hb, ha, rb, ra, cb, ca, mask_ref, *out_refs):
    step = pl.program_id(0)
    frames = ((cb.at[0], hb, ca.at[0]), (rb.at[0], f0, ra.at[0]), (rb.at[1], f1, ra.at[1]), (cb.at[1], ha, ca.at[1]))

    def region(kv, lanes):
        parts = []
        for below, own, above in frames:
            parts += [below[kv, :, lanes], own[0, kv, :, lanes], own[1, kv, :, lanes], above[kv, :, lanes]]
        return jnp.concatenate(parts, axis=0)

    scores = {}
    for h in range(heads):
        lanes = slice(h * HEAD, (h + 1) * HEAD)
        keys = region(0, lanes)
        group = keys.shape[0] // 4
        combo = combo_ref[step * heads + h]
        for f in range(2):
            q = q_ref[2 * f : 2 * f + 2, :, lanes].reshape(-1, HEAD)
            k = keys[f * group : (f + 3) * group]
            s = lax.dot_general(q, k, (((1,), (1,)), ((), ())), preferred_element_type=F32)
            scores[h, f] = s + mask_ref[combo, f]
    weights = {}
    for at, s in scores.items():
        peak = jnp.max(s, axis=1, keepdims=True)
        w = jnp.exp((s - peak) * scale)
        weights[at] = w.astype(BF16), jnp.sum(w, axis=1, keepdims=True)
    for h in range(heads):
        lanes = slice(h * HEAD, (h + 1) * HEAD)
        values = region(1, lanes)
        group = values.shape[0] // 4
        for f in range(2):
            w, total = weights[h, f]
            o = jnp.dot(w, values[f * group : (f + 3) * group], preferred_element_type=F32)
            out_refs[f][:, lanes] = (o / total).astype(BF16)


def attend(combo, chunk, qn, own, halos, masks, heads=8):
    groups, nw, inner = qn.shape
    width = own[0].shape[-1]
    lanes = heads * HEAD
    steps = width // lanes
    kv_spec = pl.BlockSpec((2, 2, nw, lanes), lambda i, *_: (0, 0, 0, i))
    return pl.pallas_call(
        functools.partial(attend_kernel, heads, HEAD**-0.5),
        grid_spec=pltpu.PrefetchScalarGridSpec(
            num_scalar_prefetch=1,
            grid=(steps,),
            in_specs=[pl.BlockSpec((groups, nw, lanes), lambda i, *_: (0, 0, chunk * steps + i))]
            + [kv_spec] * 8
            + [pl.BlockSpec(masks.shape, lambda i, *_: (0, 0, 0, 0))],
            out_specs=[pl.BlockSpec((2 * nw, lanes), lambda i, *_: (0, i))] * 2,
        ),
        out_shape=[jax.ShapeDtypeStruct((2 * nw, width), BF16)] * 2,
        compiler_params=params(),
        cost_estimate=pl.CostEstimate(flops=4 * 128 * 384 * width, bytes_accessed=32 << 20, transcendentals=0),
        name="attend",
    )(combo, qn, *own, *halos, masks)


def project_kernel(blocks, *refs):
    ins, w_ref, outs, acc = refs[:blocks], refs[blocks], refs[blocks + 1 : -1], refs[-1]
    k = pl.program_id(0)
    a = jnp.concatenate([i[...] for i in ins], axis=0)
    _, halves, cores, zs, _, _ = w_ref.shape
    w = jnp.concatenate(
        [
            jnp.concatenate([w_ref[0, n, c, z] for z in range(zs) for c in range(cores)], axis=0)
            for n in range(halves)
        ],
        axis=1,
    )
    term = jnp.dot(a, w, preferred_element_type=F32)

    @pl.when(k == 0)
    def _():
        acc[...] = term

    @pl.when(k > 0)
    def _():
        acc[...] += term

    @pl.when(k == pl.num_programs(0) - 1)
    def _():
        rows = outs[0].shape[0]
        for d, o in enumerate(outs):
            o[...] = acc[d * rows : (d + 1) * rows, :].astype(BF16)


def project(blocks, weight, zs=4):
    rows, inner = blocks[0].shape
    groups, halves, cores, depth, part, half = weight.shape
    cols, devices, inside, step = halves * half, len(blocks) // 2, depth // zs, cores * zs * part
    return pl.pallas_call(
        functools.partial(project_kernel, len(blocks)),
        grid=(groups * inside,),
        in_specs=[pl.BlockSpec((rows, step), lambda k: (0, k))] * len(blocks)
        + [pl.BlockSpec((1, halves, cores, zs, part, half), lambda k: (k // inside, 0, 0, k % inside, 0, 0))],
        out_specs=[pl.BlockSpec((2 * rows, cols), lambda k: (0, 0))] * devices,
        out_shape=[jax.ShapeDtypeStruct((2 * rows, cols), BF16)] * devices,
        scratch_shapes=[pltpu.VMEM((2 * devices * rows, cols), F32)],
        compiler_params=params(40),
        cost_estimate=pl.CostEstimate(
            flops=4 * devices * rows * inner * cols, bytes_accessed=2 * inner * cols, transcendentals=0
        ),
        name="project",
    )(*[in_hbm(b) for b in blocks], in_hbm(weight))


def finish_kernel(x_ref, hidden, gate, p0, p1, p2, p3, out):
    cols = p0.shape[-1] // 2
    for d, p in enumerate((p0, p1, p2, p3)):
        x = lax.rem(x_ref[0] + d, 4)
        for n in range(2):
            where = pl.ds(pl.multiple_of((n * 4 + x) * cols, HEAD), cols)
            term = gate[:, where] * p[:, n * cols : (n + 1) * cols].astype(F32)
            out[:, where] = (hidden[:, where].astype(F32) + term).astype(BF16)


def finish(x, hidden, gate, pieces, blocks=4):
    rows, width = hidden.shape
    step = rows // blocks
    row_spec = pl.BlockSpec((step, width), lambda i, *_: (i, 0))
    return pl.pallas_call(
        finish_kernel,
        grid_spec=pltpu.PrefetchScalarGridSpec(
            num_scalar_prefetch=1,
            grid=(blocks,),
            in_specs=[row_spec, pl.BlockSpec((1, width), lambda i, *_: (0, 0))]
            + [pl.BlockSpec((step, pieces[0].shape[1]), lambda i, *_: (i, 0))] * 4,
            out_specs=row_spec,
        ),
        out_shape=jax.ShapeDtypeStruct(hidden.shape, BF16),
        compiler_params=params(),
        name="finish",
    )(x, in_hbm(hidden), gate[None], *pieces)


def shards(hidden_in, queries, keys, values, query_gain, key_gain, reach_time, reach_rows, reach_cols, out_weight, gate):
    frames, rows, nw, inner = queries.shape
    width = hidden_in.shape[3]
    weight = lax.all_gather(out_weight, "z", axis=0, tiled=False)
    tokens = [a.reshape(frames * rows, nw, inner) for a in (queries, keys, values)]
    qn, *own = prepare(*tokens, query_gain, key_gain)
    masks = mask_tables(
        lax.axis_index(TM) * frames,
        lax.axis_index(SP) * rows,
        frames * axis_size(TM),
        rows * axis_size(SP),
        nw,
    )
    combo = reach_time * 6 + reach_rows * 3 + reach_cols
    heads = reach_time.shape[0] // CHUNKS
    outs = []
    for c in range(CHUNKS):
        f0, f1, r0, r1 = own[4 * c : 4 * c + 4]
        hb, ha = passed_along(f1, TM, 1), passed_along(f0, TM, -1)
        rb, ra = passed_along(r1, SP, 1), passed_along(r0, SP, -1)
        cb = passed_along(jnp.stack([hb[1], ha[1]]), SP, 1)
        ca = passed_along(jnp.stack([hb[0], ha[0]]), SP, -1)
        if c == 0:
            hb_in, ha_in, rb, ra, weight = lax.optimization_barrier((hb, ha, rb, ra, weight))
            weight = lax.all_gather(weight, ("y_hi", "y_lo", "core"), axis=0, tiled=False)
            weight = weight.reshape((2, 2, 2) + weight.shape[1:])
        a = attend(combo[c * heads : (c + 1) * heads], c, qn, (f0, f1), (hb_in, ha_in, rb, ra, cb, ca), masks)
        outs.append(a)
    a0, a1 = outs[0]
    left0, right1 = shifted(a0, "x", 1), shifted(a1, "x", -1)
    left1, right0 = shifted(a1, "x", 1), shifted(a0, "x", -1)
    far0, far1 = shifted(left0, "x", 1), shifted(right1, "x", -1)
    mine, near_left, near_right = project([a0, a1, left0, left1, right0, right1], weight)
    (far,) = project([far0, far1], weight)
    pieces = [mine, shifted(near_left, "x", -1), shifted(far, "x", 2), shifted(near_right, "x", 1)]
    x = lax.axis_index("x").astype(jnp.int32)[None]
    out = finish(x, hidden_in.reshape(-1, width), gate, pieces)
    return out.reshape(hidden_in.shape)


def solution(mesh):
    inner_mesh = Mesh(mesh.devices.reshape(2, 4, 2, 8, 2), TM + SP)
    tokens = P(TM, SP, None, None)
    in_specs = (tokens,) * 4 + (P(),) * 5 + (P(SP, TM), P())
    return jax.shard_map(shards, mesh=inner_mesh, in_specs=in_specs, out_specs=tokens, check_vma=False)
```

```python
import functools

import jax
import jax.numpy as jnp
from jax import lax
from jax.experimental import pallas as pl
from jax.experimental.pallas import tpu as pltpu
from jax.sharding import Mesh, PartitionSpec as P

TW = 8
HEAD = 128
TM = ("y_lo", "x")
SP = ("y_hi", "z", "core")
CHUNKS = 1
COMBOS = 12
F32, BF16 = jnp.float32, jnp.bfloat16


def axis_size(axes):
    n = 1
    for a in axes:
        n *= lax.axis_size(a)
    return n


def passed_along(block, axes, distance):
    n = axis_size(axes)
    route = [(i - distance, i) for i in range(n) if 0 <= i - distance < n]
    return lax.ppermute(block, axes, route)


def shifted(block, axis, distance):
    n = lax.axis_size(axis)
    return lax.ppermute(block, axis, [(i, (i + distance) % n) for i in range(n)])


def in_hbm(array):
    return pltpu.with_memory_space_constraint(array, pltpu.HBM)


def params(megabytes=24):
    return pltpu.CompilerParams(vmem_limit_bytes=megabytes << 20)


def prepare_kernel(q_ref, k_ref, v_ref, qg_ref, kg_ref, qn_ref, *outs):
    i = pl.program_id(0)
    f, r = i // 2, i % 2
    inner = q_ref.shape[-1]

    def normed(ref, gain):
        a = ref[0].astype(F32)
        ms = jnp.sum(a * a, axis=-1, keepdims=True) * (1.0 / inner)
        return (a * lax.rsqrt(ms + 1e-06) * gain[...]).astype(BF16)

    qn_ref[0] = normed(q_ref, qg_ref)
    kn = normed(k_ref, kg_ref)
    v = v_ref[0]
    width = inner // (len(outs) // 4)
    for c in range(len(outs) // 4):
        f0, f1, r0, r1 = outs[4 * c : 4 * c + 4]
        lanes = slice(c * width, (c + 1) * width)
        for which, ref in ((0, f0), (1, f1)):

            @pl.when(f == which)
            def _(ref=ref):
                ref[0, 0] = kn[:, lanes]
                ref[0, 1] = v[:, lanes]

        for which, ref in ((0, r0), (1, r1)):

            @pl.when(r == which)
            def _(ref=ref):
                ref[0, 0] = kn[:, lanes]
                ref[0, 1] = v[:, lanes]


def prepare(queries, keys, values, query_gain, key_gain):
    groups, nw, inner = queries.shape
    width = inner // CHUNKS
    token_spec = pl.BlockSpec((1, nw, inner), lambda i: (i, 0, 0))
    gain_spec = pl.BlockSpec((1, inner), lambda i: (0, 0))
    out_shape = [pltpu.HBM(queries.shape, BF16)]
    out_specs = [token_spec]
    for _ in range(CHUNKS):
        out_shape += [pltpu.HBM((2, 2, nw, width), BF16)] * 4
        out_specs += [
            pl.BlockSpec((1, 2, nw, width), lambda i: (jnp.minimum(i, 1), 0, 0, 0)),
            pl.BlockSpec((1, 2, nw, width), lambda i: (jnp.maximum(i - 2, 0), 0, 0, 0)),
            pl.BlockSpec((1, 2, nw, width), lambda i: (i // 2, 0, 0, 0)),
            pl.BlockSpec((1, 2, nw, width), lambda i: (i // 2, 0, 0, 0)),
        ]
    return pl.pallas_call(
        prepare_kernel,
        grid=(groups,),
        in_specs=[token_spec] * 3 + [gain_spec] * 2,
        out_specs=out_specs,
        out_shape=out_shape,
        compiler_params=params(),
        cost_estimate=pl.CostEstimate(flops=0, bytes_accessed=12 << 20, transcendentals=0),
        name="prepare",
    )(*[in_hbm(a) for a in (queries, keys, values)], query_gain[None], key_gain[None])


def mask_tables(first_frame, first_row, frame_count, row_count, nw):
    i32 = jnp.int32
    shape = (COMBOS, 2, 2 * nw, 3 * 4 * nw)
    t = lax.broadcasted_iota(i32, shape, 0)
    f = lax.broadcasted_iota(i32, shape, 1)
    q = lax.broadcasted_iota(i32, shape, 2)
    k = lax.broadcasted_iota(i32, shape, 3)
    kf, kr, kc = k // (4 * nw), k // nw % 4, k % nw
    frame, row = first_frame - 1 + f + kf, first_row - 1 + kr
    allowed = jnp.abs(kf - 1) <= t // 6
    allowed &= jnp.abs(q // nw + 1 - kr) <= t // 3 % 2
    allowed &= jnp.abs(q % nw // TW - kc // TW) <= t % 3
    allowed &= (frame >= 0) & (frame < frame_count) & (row >= 0) & (row < row_count)
    return jnp.where(allowed, 0.0, -jnp.inf).astype(F32)


def attend_kernel(heads, scale, combo_ref, q_ref, f0, f1, hb, ha, rb, ra, cb, ca, mask_ref, *out_refs):
    step = pl.program_id(0)
    frames = ((cb.at[0], hb, ca.at[0]), (rb.at[0], f0, ra.at[0]), (rb.at[1], f1, ra.at[1]), (cb.at[1], ha, ca.at[1]))

    def region(kv, lanes):
        parts = []
        for below, own, above in frames:
            parts += [below[kv, :, lanes], own[0, kv, :, lanes], own[1, kv, :, lanes], above[kv, :, lanes]]
        return jnp.concatenate(parts, axis=0)

    scores = {}
    for h in range(heads):
        lanes = slice(h * HEAD, (h + 1) * HEAD)
        keys = region(0, lanes)
        group = keys.shape[0] // 4
        combo = combo_ref[step * heads + h]
        for f in range(2):
            q = q_ref[2 * f : 2 * f + 2, :, lanes].reshape(-1, HEAD)
            k = keys[f * group : (f + 3) * group]
            s = lax.dot_general(q, k, (((1,), (1,)), ((), ())), preferred_element_type=F32)
            scores[h, f] = s + mask_ref[combo, f]
    weights = {}
    for at, s in scores.items():
        peak = jnp.max(s, axis=1, keepdims=True)
        w = jnp.exp((s - peak) * scale)
        weights[at] = w.astype(BF16), jnp.sum(w, axis=1, keepdims=True)
    for h in range(heads):
        lanes = slice(h * HEAD, (h + 1) * HEAD)
        values = region(1, lanes)
        group = values.shape[0] // 4
        for f in range(2):
            w, total = weights[h, f]
            o = jnp.dot(w, values[f * group : (f + 3) * group], preferred_element_type=F32)
            out_refs[f][:, lanes] = (o / total).astype(BF16)


def attend(combo, chunk, qn, own, halos, masks, heads=8):
    groups, nw, inner = qn.shape
    width = own[0].shape[-1]
    lanes = heads * HEAD
    steps = width // lanes
    kv_spec = pl.BlockSpec((2, 2, nw, lanes), lambda i, *_: (0, 0, 0, i))
    return pl.pallas_call(
        functools.partial(attend_kernel, heads, HEAD**-0.5),
        grid_spec=pltpu.PrefetchScalarGridSpec(
            num_scalar_prefetch=1,
            grid=(steps,),
            in_specs=[pl.BlockSpec((groups, nw, lanes), lambda i, *_: (0, 0, chunk * steps + i))]
            + [kv_spec] * 8
            + [pl.BlockSpec(masks.shape, lambda i, *_: (0, 0, 0, 0))],
            out_specs=[pl.BlockSpec((2 * nw, lanes), lambda i, *_: (0, i))] * 2,
        ),
        out_shape=[pltpu.HBM((2 * nw, width), BF16)] * 2,
        compiler_params=params(),
        cost_estimate=pl.CostEstimate(flops=4 * 128 * 384 * width, bytes_accessed=32 << 20, transcendentals=0),
        name="attend",
    )(combo, qn, *own, *halos, masks)


def project_kernel(blocks, *refs):
    ins, w_ref, outs, acc = refs[:blocks], refs[blocks], refs[blocks + 1 : -1], refs[-1]
    k = pl.program_id(0)
    a = jnp.concatenate([i[...] for i in ins], axis=0)
    _, halves, cores, zs, _, _ = w_ref.shape
    w = jnp.concatenate(
        [
            jnp.concatenate([w_ref[0, n, c, z] for z in range(zs) for c in range(cores)], axis=0)
            for n in range(halves)
        ],
        axis=1,
    )
    term = jnp.dot(a, w, preferred_element_type=F32)

    @pl.when(k == 0)
    def _():
        acc[...] = term

    @pl.when(k > 0)
    def _():
        acc[...] += term

    @pl.when(k == pl.num_programs(0) - 1)
    def _():
        rows = outs[0].shape[0]
        for d, o in enumerate(outs):
            o[...] = acc[d * rows : (d + 1) * rows, :].astype(BF16)


def project(blocks, weight, zs=4):
    rows, inner = blocks[0].shape
    groups, halves, cores, depth, part, half = weight.shape
    cols, devices, inside, step = halves * half, len(blocks) // 2, depth // zs, cores * zs * part
    return pl.pallas_call(
        functools.partial(project_kernel, len(blocks)),
        grid=(groups * inside,),
        in_specs=[pl.BlockSpec((rows, step), lambda k: (0, k))] * len(blocks)
        + [pl.BlockSpec((1, halves, cores, zs, part, half), lambda k: (k // inside, 0, 0, k % inside, 0, 0))],
        out_specs=[pl.BlockSpec((2 * rows, cols), lambda k: (0, 0))] * devices,
        out_shape=[jax.ShapeDtypeStruct((2 * rows, cols), BF16)] * devices,
        scratch_shapes=[pltpu.VMEM((2 * devices * rows, cols), F32)],
        compiler_params=params(40),
        cost_estimate=pl.CostEstimate(
            flops=4 * devices * rows * inner * cols, bytes_accessed=2 * inner * cols, transcendentals=0
        ),
        name="project",
    )(*blocks, in_hbm(weight))


def finish_kernel(x_ref, hidden, gate, p0, p1, p2, p3, out):
    cols = p0.shape[-1] // 2
    for d, p in enumerate((p0, p1, p2, p3)):
        x = lax.rem(x_ref[0] + d, 4)
        for n in range(2):
            where = pl.ds(pl.multiple_of((n * 4 + x) * cols, HEAD), cols)
            term = gate[:, where] * p[:, n * cols : (n + 1) * cols].astype(F32)
            out[:, where] = (hidden[:, where].astype(F32) + term).astype(BF16)


def finish(x, hidden, gate, pieces, blocks=4):
    rows, width = hidden.shape
    step = rows // blocks
    row_spec = pl.BlockSpec((step, width), lambda i, *_: (i, 0))
    return pl.pallas_call(
        finish_kernel,
        grid_spec=pltpu.PrefetchScalarGridSpec(
            num_scalar_prefetch=1,
            grid=(blocks,),
            in_specs=[row_spec, pl.BlockSpec((1, width), lambda i, *_: (0, 0))]
            + [pl.BlockSpec((step, pieces[0].shape[1]), lambda i, *_: (i, 0))] * 4,
            out_specs=row_spec,
        ),
        out_shape=jax.ShapeDtypeStruct(hidden.shape, BF16),
        compiler_params=params(),
        name="finish",
    )(x, hidden, gate[None], *pieces)


def shards(hidden_in, queries, keys, values, query_gain, key_gain, reach_time, reach_rows, reach_cols, out_weight, gate):
    frames, rows, nw, inner = queries.shape
    width = hidden_in.shape[3]
    weight = lax.all_gather(out_weight, "z", axis=0, tiled=False)
    tokens = [a.reshape(frames * rows, nw, inner) for a in (queries, keys, values)]
    qn, *own = prepare(*tokens, query_gain, key_gain)
    masks = mask_tables(
        lax.axis_index(TM) * frames,
        lax.axis_index(SP) * rows,
        frames * axis_size(TM),
        rows * axis_size(SP),
        nw,
    )
    combo = reach_time * 6 + reach_rows * 3 + reach_cols
    heads = reach_time.shape[0] // CHUNKS
    outs = []
    for c in range(CHUNKS):
        f0, f1, r0, r1 = own[4 * c : 4 * c + 4]
        hb, ha = passed_along(f1, TM, 1), passed_along(f0, TM, -1)
        if c == 0:
            hb, ha, r0, r1, weight = lax.optimization_barrier((hb, ha, r0, r1, weight))
            weight = lax.all_gather(weight, ("y_hi", "y_lo", "core"), axis=0, tiled=False)
            weight = weight.reshape((2, 2, 2) + weight.shape[1:])
        cb = passed_along(jnp.stack([hb[1], ha[1]]), SP, 1)
        ca = passed_along(jnp.stack([hb[0], ha[0]]), SP, -1)
        rb, ra = passed_along(r1, SP, 1), passed_along(r0, SP, -1)
        a = attend(combo[c * heads : (c + 1) * heads], c, qn, (f0, f1), (hb, ha, rb, ra, cb, ca), masks)
        outs.append(a)
    a0, a1 = outs[0]
    left0, right1 = shifted(a0, "x", 1), shifted(a1, "x", -1)
    left1, right0 = shifted(a1, "x", 1), shifted(a0, "x", -1)
    far0, far1 = shifted(left0, "x", 1), shifted(right1, "x", -1)
    far, near_left, near_right = project([far0, far1, left0, left1, right0, right1], weight)
    a0, far = lax.optimization_barrier((a0, far))
    (mine,) = project([a0, a1], weight)
    pieces = [mine, shifted(near_left, "x", -1), shifted(far, "x", 2), shifted(near_right, "x", 1)]
    x = lax.axis_index("x").astype(jnp.int32)[None]
    out = finish(x, hidden_in.reshape(-1, width), gate, pieces)
    return out.reshape(hidden_in.shape)


def solution(mesh):
    inner_mesh = Mesh(mesh.devices.reshape(2, 4, 2, 8, 2), TM + SP)
    tokens = P(TM, SP, None, None)
    in_specs = (tokens,) * 4 + (P(),) * 5 + (P(SP, TM), P())
    return jax.shard_map(shards, mesh=inner_mesh, in_specs=in_specs, out_specs=tokens, check_vma=False)
```

```python
import functools

import jax
import jax.numpy as jnp
from jax import lax
from jax.experimental import pallas as pl
from jax.experimental.pallas import tpu as pltpu
from jax.sharding import Mesh, PartitionSpec as P

TW = 8
HEAD = 128
TM = ("y_lo", "x")
SP = ("y_hi", "z", "core")
CHUNKS = 2
COMBOS = 12
F32, BF16 = jnp.float32, jnp.bfloat16


def axis_size(axes):
    n = 1
    for a in axes:
        n *= lax.axis_size(a)
    return n


def passed_along(block, axes, distance):
    n = axis_size(axes)
    route = [(i - distance, i) for i in range(n) if 0 <= i - distance < n]
    return lax.ppermute(block, axes, route)


def shifted(block, axis, distance):
    n = lax.axis_size(axis)
    return lax.ppermute(block, axis, [(i, (i + distance) % n) for i in range(n)])


def along_y(block, distance):
    at = lambda y: (y % 2) * 2 + y // 2
    return lax.ppermute(block, ("y_lo", "y_hi"), [(at(y), at((y + distance) % 4)) for y in range(4)])


def in_hbm(array):
    return pltpu.with_memory_space_constraint(array, pltpu.HBM)


def params(megabytes=24):
    return pltpu.CompilerParams(vmem_limit_bytes=megabytes << 20)


def prepare_kernel(q_ref, k_ref, v_ref, qg_ref, kg_ref, qn_ref, *outs):
    i = pl.program_id(0)
    f, r = i // 2, i % 2
    inner = q_ref.shape[-1]

    def normed(ref, gain):
        a = ref[0].astype(F32)
        ms = jnp.sum(a * a, axis=-1, keepdims=True) * (1.0 / inner)
        return (a * lax.rsqrt(ms + 1e-06) * gain[...]).astype(BF16)

    qn_ref[0] = normed(q_ref, qg_ref)
    kn = normed(k_ref, kg_ref)
    v = v_ref[0]
    for which, ref in ((0, outs[0]), (1, outs[1])):

        @pl.when(r == which)
        def _(ref=ref):
            ref[0, 0] = kn
            ref[0, 1] = v

    width = inner // CHUNKS
    for c in range(CHUNKS):
        lanes = slice(c * width, (c + 1) * width)
        for which, ref in ((0, outs[2 + 2 * c]), (1, outs[3 + 2 * c])):

            @pl.when(f == which)
            def _(ref=ref):
                ref[0, 0] = kn[:, lanes]
                ref[0, 1] = v[:, lanes]


def prepare(queries, keys, values, query_gain, key_gain):
    groups, nw, inner = queries.shape
    width = inner // CHUNKS
    token_spec = pl.BlockSpec((1, nw, inner), lambda i: (i, 0, 0))
    gain_spec = pl.BlockSpec((1, inner), lambda i: (0, 0))
    out_shape = [pltpu.HBM(queries.shape, BF16)] + [pltpu.HBM((2, 2, nw, inner), BF16)] * 2
    out_specs = [token_spec] + [pl.BlockSpec((1, 2, nw, inner), lambda i: (i // 2, 0, 0, 0))] * 2
    for _ in range(CHUNKS):
        out_shape += [pltpu.HBM((2, 2, nw, width), BF16)] * 2
        out_specs += [
            pl.BlockSpec((1, 2, nw, width), lambda i: (jnp.minimum(i, 1), 0, 0, 0)),
            pl.BlockSpec((1, 2, nw, width), lambda i: (jnp.maximum(i - 2, 0), 0, 0, 0)),
        ]
    return pl.pallas_call(
        prepare_kernel,
        grid=(groups,),
        in_specs=[token_spec] * 3 + [gain_spec] * 2,
        out_specs=out_specs,
        out_shape=out_shape,
        compiler_params=params(),
        cost_estimate=pl.CostEstimate(flops=0, bytes_accessed=12 << 20, transcendentals=0),
        name="prepare",
    )(*[in_hbm(a) for a in (queries, keys, values)], query_gain[None], key_gain[None])


def mask_tables(first_frame, first_row, frame_count, row_count, nw):
    i32 = jnp.int32
    shape = (COMBOS, 2, 2 * nw, 3 * 4 * nw)
    t = lax.broadcasted_iota(i32, shape, 0)
    f = lax.broadcasted_iota(i32, shape, 1)
    q = lax.broadcasted_iota(i32, shape, 2)
    k = lax.broadcasted_iota(i32, shape, 3)
    kf, kr, kc = k // (4 * nw), k // nw % 4, k % nw
    frame, row = first_frame - 1 + f + kf, first_row - 1 + kr
    allowed = jnp.abs(kf - 1) <= t // 6
    allowed &= jnp.abs(q // nw + 1 - kr) <= t // 3 % 2
    allowed &= jnp.abs(q % nw // TW - kc // TW) <= t % 3
    allowed &= (frame >= 0) & (frame < frame_count) & (row >= 0) & (row < row_count)
    return jnp.where(allowed, 0.0, -jnp.inf).astype(F32)


def attend_kernel(heads, scale, combo_ref, q_ref, f0, f1, hb, ha, rb, ra, cb, ca, mask_ref, out_ref):
    step = pl.program_id(0)
    frames = ((cb.at[0], hb, ca.at[0]), (rb.at[0], f0, ra.at[0]), (rb.at[1], f1, ra.at[1]), (cb.at[1], ha, ca.at[1]))

    def region(kv, lanes):
        parts = []
        for below, own, above in frames:
            parts += [below[kv, :, lanes], own[0, kv, :, lanes], own[1, kv, :, lanes], above[kv, :, lanes]]
        return jnp.concatenate(parts, axis=0)

    scores = {}
    for h in range(heads):
        lanes = slice(h * HEAD, (h + 1) * HEAD)
        keys = region(0, lanes)
        group = keys.shape[0] // 4
        combo = combo_ref[step * heads + h]
        for f in range(2):
            q = q_ref[2 * f : 2 * f + 2, :, lanes].reshape(-1, HEAD)
            k = keys[f * group : (f + 3) * group]
            s = lax.dot_general(q, k, (((1,), (1,)), ((), ())), preferred_element_type=F32)
            scores[h, f] = s + mask_ref[combo, f]
    weights = {}
    for at, s in scores.items():
        peak = jnp.max(s, axis=1, keepdims=True)
        w = jnp.exp((s - peak) * scale)
        weights[at] = w.astype(BF16), jnp.sum(w, axis=1, keepdims=True)
    for h in range(heads):
        lanes = slice(h * HEAD, (h + 1) * HEAD)
        values = region(1, lanes)
        group = values.shape[0] // 4
        for f in range(2):
            w, total = weights[h, f]
            o = jnp.dot(w, values[f * group : (f + 3) * group], preferred_element_type=F32)
            out_ref[f, :, lanes] = (o / total).astype(BF16)


def attend(combo, chunk, qn, own, frames, rows, corners, masks, heads=10):
    groups, nw, inner = qn.shape
    width = own[0].shape[-1]
    lanes = heads * HEAD
    steps = width // lanes
    kv_spec = pl.BlockSpec((2, 2, nw, lanes), lambda i, *_: (0, 0, 0, i))
    row_spec = pl.BlockSpec((2, 2, nw, lanes), lambda i, *_: (0, 0, 0, chunk * steps + i))
    return pl.pallas_call(
        functools.partial(attend_kernel, heads, HEAD**-0.5),
        grid_spec=pltpu.PrefetchScalarGridSpec(
            num_scalar_prefetch=1,
            grid=(steps,),
            in_specs=[pl.BlockSpec((groups, nw, lanes), lambda i, *_: (0, 0, chunk * steps + i))]
            + [kv_spec] * 4
            + [row_spec] * 2
            + [kv_spec] * 2
            + [pl.BlockSpec(masks.shape, lambda i, *_: (0, 0, 0, 0))],
            out_specs=pl.BlockSpec((2, 2 * nw, lanes), lambda i, *_: (0, 0, i)),
        ),
        out_shape=pltpu.HBM((2, 2 * nw, width), BF16),
        compiler_params=params(),
        cost_estimate=pl.CostEstimate(flops=4 * 128 * 384 * width, bytes_accessed=32 << 20, transcendentals=0),
        name="attend",
    )(combo, qn, *own, *frames, *rows, *corners, masks)


def project_kernel(inside, blocks, _, *refs):
    ins, (w0, w1), outs, (acc, a_buf) = refs[:blocks], refs[blocks : blocks + 2], refs[blocks + 2 : -2], refs[-2:]
    k = pl.program_id(0)
    for c in range(CHUNKS):

        @pl.when(k // inside == c)
        def _(c=c):
            of_chunk = ins[c * (blocks // CHUNKS) : (c + 1) * (blocks // CHUNKS)]
            a_buf[...] = jnp.concatenate([i[...].reshape(-1, i.shape[-1]) for i in of_chunk], axis=0)

    zs, cores = w0.shape[:2]
    w = jnp.concatenate(
        [jnp.concatenate([w_ref[z, c, 0] for z in range(zs) for c in range(cores)], axis=0) for w_ref in (w0, w1)],
        axis=1,
    )
    term = jnp.dot(a_buf[...], w, preferred_element_type=F32)

    @pl.when(k == 0)
    def _():
        acc[...] = term

    @pl.when(k > 0)
    def _():
        acc[...] += term

    @pl.when(k == pl.num_programs(0) - 1)
    def _():
        rows = outs[0].shape[0]
        for d, o in enumerate(outs):
            o[...] = acc[d * rows : (d + 1) * rows, :].astype(BF16)


def project(y, chunks, weight, rows=128, zs=4):
    depth, cores, ys, part, half = weight.shape
    step, inside = cores * zs * part, depth // zs
    steps = 2 * inside
    inside_chunk = steps // CHUNKS
    blocks = [b for blocks in chunks for b in blocks]
    tokens = sum(b.shape[0] * b.shape[1] for b in chunks[0])
    devices, cols = tokens // rows, 2 * half

    def block_spec(c, b):
        return pl.BlockSpec(
            b.shape[:2] + (step,), lambda k, _: (0, 0, jnp.clip(k - c * inside_chunk, 0, inside_chunk - 1))
        )

    def weight_spec(y_lo):
        return pl.BlockSpec(
            (zs, cores, 1, part, half),
            lambda k, y_ref: (k % inside, 0, lax.rem(y_ref[0] + ys - (2 * (k // inside) + y_lo), ys), 0, 0),
        )

    weight = in_hbm(weight)
    return pl.pallas_call(
        functools.partial(project_kernel, inside_chunk, len(blocks)),
        grid_spec=pltpu.PrefetchScalarGridSpec(
            num_scalar_prefetch=1,
            grid=(steps,),
            in_specs=[block_spec(c, b) for c, blocks in enumerate(chunks) for b in blocks]
            + [weight_spec(0), weight_spec(1)],
            out_specs=[pl.BlockSpec((rows, cols), lambda k, _: (0, 0))] * devices,
            scratch_shapes=[pltpu.VMEM((tokens, cols), F32), pltpu.VMEM((tokens, step), BF16)],
        ),
        out_shape=[jax.ShapeDtypeStruct((rows, cols), BF16)] * devices,
        compiler_params=params(28),
        cost_estimate=pl.CostEstimate(
            flops=2 * tokens * step * steps * cols, bytes_accessed=2 * step * steps * cols, transcendentals=0
        ),
        name="project",
    )(y, *blocks, weight, weight)


def finish_kernel(x_ref, hidden, gate, p0, p1, p2, p3, out):
    cols = p0.shape[-1] // 2
    for d, p in enumerate((p0, p1, p2, p3)):
        x = lax.rem(x_ref[0] + d, 4)
        for n in range(2):
            where = pl.ds(pl.multiple_of((n * 4 + x) * cols, HEAD), cols)
            term = gate[:, where] * p[:, n * cols : (n + 1) * cols].astype(F32)
            out[:, where] = (hidden[:, where].astype(F32) + term).astype(BF16)


def finish(x, hidden, gate, pieces, blocks=4):
    rows, width = hidden.shape
    step = rows // blocks
    row_spec = pl.BlockSpec((step, width), lambda i, *_: (i, 0))
    return pl.pallas_call(
        finish_kernel,
        grid_spec=pltpu.PrefetchScalarGridSpec(
            num_scalar_prefetch=1,
            grid=(blocks,),
            in_specs=[row_spec, pl.BlockSpec((1, width), lambda i, *_: (0, 0))]
            + [pl.BlockSpec((step, pieces[0].shape[1]), lambda i, *_: (i, 0))] * 4,
            out_specs=row_spec,
        ),
        out_shape=jax.ShapeDtypeStruct(hidden.shape, BF16),
        compiler_params=params(),
        name="finish",
    )(x, hidden, gate[None], *pieces)


def shards(hidden_in, queries, keys, values, query_gain, key_gain, reach_time, reach_rows, reach_cols, out_weight, gate):
    frames, rows, nw, inner = queries.shape
    width = hidden_in.shape[3]
    near_weights = [out_weight] + [along_y(out_weight, d) for d in (1, 2, 3)]

    tokens = [a.reshape(frames * rows, nw, inner) for a in (queries, keys, values)]
    qn, r0, r1, *own = prepare(*tokens, query_gain, key_gain)
    *near_weights, qn = lax.optimization_barrier((*near_weights, qn))
    weight = lax.all_gather(jnp.stack(near_weights), ("z", "core"), axis=0, tiled=False)
    weight = weight.reshape((lax.axis_size("z"), lax.axis_size("core")) + weight.shape[1:])
    masks = mask_tables(
        lax.axis_index(TM) * frames,
        lax.axis_index(SP) * rows,
        frames * axis_size(TM),
        rows * axis_size(SP),
        nw,
    )
    combo = reach_time * 6 + reach_rows * 3 + reach_cols
    heads = reach_time.shape[0] // CHUNKS
    rb, ra = passed_along(r1, SP, 1), passed_along(r0, SP, -1)
    mine, near, hb, a = [], [], None, None
    for c in range(CHUNKS):
        f0, f1 = own[2 * c : 2 * c + 2]
        hb, ha = passed_along(f1, TM, 1), passed_along(f0, TM, -1)
        corner_b, corner_a = hb, ha
        if c:
            corner_b, corner_a, a = lax.optimization_barrier((hb, ha, a))
            mine[-1] = a
        to_above = jnp.stack([corner_b[1], corner_a[1]])
        if c == 0:
            to_above, rb = lax.optimization_barrier((to_above, rb))
        cb = passed_along(to_above, SP, 1)
        ca = passed_along(jnp.stack([corner_b[0], corner_a[0]]), SP, -1)
        a = attend(
            combo[c * heads : (c + 1) * heads], c, qn, (f0, f1), (hb, ha), (rb, ra), (cb, ca), masks
        )
        mine.append(a)
    for a in mine:
        left, right = shifted(a, "x", 1), shifted(a, "x", -1)
        far0, far1 = shifted(left[:1], "x", 1), shifted(right[1:], "x", -1)
        near.append([far0, far1, left, right])
    y = (2 * lax.axis_index("y_hi") + lax.axis_index("y_lo")).astype(jnp.int32)[None]
    far, near_left, near_right = project(y, near, weight)
    mine[0], far = lax.optimization_barrier((mine[0], far))
    (mine,) = project(y, [[a] for a in mine], weight)
    pieces = [mine, shifted(near_left, "x", -1), shifted(far, "x", 2), shifted(near_right, "x", 1)]
    x = lax.axis_index("x").astype(jnp.int32)[None]
    out = finish(x, hidden_in.reshape(-1, width), gate, pieces)
    return out.reshape(hidden_in.shape)


def solution(mesh):
    inner_mesh = Mesh(mesh.devices.reshape(2, 4, 2, 8, 2), TM + SP)
    tokens = P(TM, SP, None, None)
    in_specs = (tokens,) * 4 + (P(),) * 5 + (P(SP, TM), P())
    return jax.shard_map(shards, mesh=inner_mesh, in_specs=in_specs, out_specs=tokens, check_vma=False)
```

```python
import functools

import jax
import jax.numpy as jnp
from jax import lax
from jax.experimental import pallas as pl
from jax.experimental.pallas import tpu as pltpu
from jax.sharding import Mesh, PartitionSpec as P

TW = 8
HEAD = 128
TM = ("y_lo", "x")
SP = ("y_hi", "z", "core")
CHUNKS = 2
COMBOS = 12
F32, BF16 = jnp.float32, jnp.bfloat16


def axis_size(axes):
    n = 1
    for a in axes:
        n *= lax.axis_size(a)
    return n


def passed_along(block, axes, distance):
    n = axis_size(axes)
    route = [(i - distance, i) for i in range(n) if 0 <= i - distance < n]
    return lax.ppermute(block, axes, route)


def shifted(block, axis, distance):
    n = lax.axis_size(axis)
    return lax.ppermute(block, axis, [(i, (i + distance) % n) for i in range(n)])


def in_hbm(array):
    return pltpu.with_memory_space_constraint(array, pltpu.HBM)


def params(megabytes=60):
    return pltpu.CompilerParams(vmem_limit_bytes=megabytes << 20)


def prepare_kernel(q_ref, k_ref, v_ref, qg_ref, kg_ref, qn_ref, *outs):
    i = pl.program_id(0)
    f, r = i // 2, i % 2
    inner = q_ref.shape[-1]

    def normed(ref, gain):
        a = ref[0].astype(F32)
        ms = jnp.sum(a * a, axis=-1, keepdims=True) * (1.0 / inner)
        return (a * lax.rsqrt(ms + 1e-06) * gain[...]).astype(BF16)

    qn_ref[0] = normed(q_ref, qg_ref)
    kn = normed(k_ref, kg_ref)
    v = v_ref[0]
    for which, ref in ((0, outs[0]), (1, outs[1])):

        @pl.when(r == which)
        def _(ref=ref):
            ref[0, 0] = kn
            ref[0, 1] = v

    width = inner // CHUNKS
    for c in range(CHUNKS):
        lanes = slice(c * width, (c + 1) * width)
        for which, ref in ((0, outs[2 + 2 * c]), (1, outs[3 + 2 * c])):

            @pl.when(f == which)
            def _(ref=ref):
                ref[0, 0] = kn[:, lanes]
                ref[0, 1] = v[:, lanes]


def prepare(queries, keys, values, query_gain, key_gain):
    groups, nw, inner = queries.shape
    width = inner // CHUNKS
    token_spec = pl.BlockSpec((1, nw, inner), lambda i: (i, 0, 0))
    gain_spec = pl.BlockSpec((1, inner), lambda i: (0, 0))
    out_shape = [pltpu.HBM(queries.shape, BF16)] + [pltpu.HBM((2, 2, nw, inner), BF16)] * 2
    out_specs = [token_spec] + [pl.BlockSpec((1, 2, nw, inner), lambda i: (i // 2, 0, 0, 0))] * 2
    for _ in range(CHUNKS):
        out_shape += [pltpu.HBM((2, 2, nw, width), BF16)] * 2
        out_specs += [
            pl.BlockSpec((1, 2, nw, width), lambda i: (jnp.minimum(i, 1), 0, 0, 0)),
            pl.BlockSpec((1, 2, nw, width), lambda i: (jnp.maximum(i - 2, 0), 0, 0, 0)),
        ]
    return pl.pallas_call(
        prepare_kernel,
        grid=(groups,),
        in_specs=[token_spec] * 3 + [gain_spec] * 2,
        out_specs=out_specs,
        out_shape=out_shape,
        compiler_params=params(),
        cost_estimate=pl.CostEstimate(flops=0, bytes_accessed=12 << 20, transcendentals=0),
        name="prepare",
    )(*[in_hbm(a) for a in (queries, keys, values)], query_gain[None], key_gain[None])


def mask_tables(first_frame, first_row, frame_count, row_count, nw):
    i32 = jnp.int32
    shape = (COMBOS, 2, 2 * nw, 3 * 4 * nw)
    t = lax.broadcasted_iota(i32, shape, 0)
    f = lax.broadcasted_iota(i32, shape, 1)
    q = lax.broadcasted_iota(i32, shape, 2)
    k = lax.broadcasted_iota(i32, shape, 3)
    kf, kr, kc = k // (4 * nw), k // nw % 4, k % nw
    frame, row = first_frame - 1 + f + kf, first_row - 1 + kr
    allowed = jnp.abs(kf - 1) <= t // 6
    allowed &= jnp.abs(q // nw + 1 - kr) <= t // 3 % 2
    allowed &= jnp.abs(q % nw // TW - kc // TW) <= t % 3
    allowed &= (frame >= 0) & (frame < frame_count) & (row >= 0) & (row < row_count)
    return jnp.where(allowed, 0.0, -jnp.inf).astype(F32)


def attend_kernel(heads, scale, combo_ref, q_ref, f0, f1, hb, ha, rb, ra, cb, ca, mask_ref, out_ref):
    step = pl.program_id(0)
    frames = ((cb.at[0], hb, ca.at[0]), (rb.at[0], f0, ra.at[0]), (rb.at[1], f1, ra.at[1]), (cb.at[1], ha, ca.at[1]))

    def region(kv, lanes):
        parts = []
        for below, own, above in frames:
            parts += [below[kv, :, lanes], own[0, kv, :, lanes], own[1, kv, :, lanes], above[kv, :, lanes]]
        return jnp.concatenate(parts, axis=0)

    scores = {}
    for h in range(heads):
        lanes = slice(h * HEAD, (h + 1) * HEAD)
        keys = region(0, lanes)
        group = keys.shape[0] // 4
        combo = combo_ref[step * heads + h]
        for f in range(2):
            q = q_ref[2 * f : 2 * f + 2, :, lanes].reshape(-1, HEAD)
            k = keys[f * group : (f + 3) * group]
            s = lax.dot_general(q, k, (((1,), (1,)), ((), ())), preferred_element_type=F32)
            scores[h, f] = s + mask_ref[combo, f]
    weights = {}
    for at, s in scores.items():
        peak = jnp.max(s, axis=1, keepdims=True)
        w = jnp.exp((s - peak) * scale)
        weights[at] = w.astype(BF16), jnp.sum(w, axis=1, keepdims=True)
    for h in range(heads):
        lanes = slice(h * HEAD, (h + 1) * HEAD)
        values = region(1, lanes)
        group = values.shape[0] // 4
        for f in range(2):
            w, total = weights[h, f]
            o = jnp.dot(w, values[f * group : (f + 3) * group], preferred_element_type=F32)
            out_ref[f, :, lanes] = (o / total).astype(BF16)


def attend(combo, chunk, qn, own, frames, rows, corners, masks, heads=10):
    groups, nw, inner = qn.shape
    width = own[0].shape[-1]
    lanes = heads * HEAD
    steps = width // lanes
    kv_spec = pl.BlockSpec((2, 2, nw, lanes), lambda i, *_: (0, 0, 0, i))
    row_spec = pl.BlockSpec((2, 2, nw, lanes), lambda i, *_: (0, 0, 0, chunk * steps + i))
    return pl.pallas_call(
        functools.partial(attend_kernel, heads, HEAD**-0.5),
        grid_spec=pltpu.PrefetchScalarGridSpec(
            num_scalar_prefetch=1,
            grid=(steps,),
            in_specs=[pl.BlockSpec((groups, nw, lanes), lambda i, *_: (0, 0, chunk * steps + i))]
            + [kv_spec] * 4
            + [row_spec] * 2
            + [kv_spec] * 2
            + [pl.BlockSpec(masks.shape, lambda i, *_: (0, 0, 0, 0))],
            out_specs=pl.BlockSpec((2, 2 * nw, lanes), lambda i, *_: (0, 0, i)),
        ),
        out_shape=pltpu.HBM((2, 2 * nw, width), BF16),
        compiler_params=params(),
        cost_estimate=pl.CostEstimate(flops=4 * 128 * 384 * width, bytes_accessed=32 << 20, transcendentals=0),
        name="attend",
    )(combo, qn, *own, *frames, *rows, *corners, masks)


def project_kernel(inside, blocks, *refs):
    ins, w_ref, outs, (acc, a_buf) = refs[:blocks], refs[blocks], refs[blocks + 1 : -2], refs[-2:]
    k = pl.program_id(0)
    for c in range(CHUNKS):

        @pl.when(k // inside == c)
        def _(c=c):
            of_chunk = ins[c * (blocks // CHUNKS) : (c + 1) * (blocks // CHUNKS)]
            a_buf[...] = jnp.concatenate([i[...].reshape(-1, i.shape[-1]) for i in of_chunk], axis=0)

    _, halves, cores, zs, _, _ = w_ref.shape
    w = jnp.concatenate(
        [
            jnp.concatenate([w_ref[0, n, c, z] for z in range(zs) for c in range(cores)], axis=0)
            for n in range(halves)
        ],
        axis=1,
    )
    term = jnp.dot(a_buf[...], w, preferred_element_type=F32)

    @pl.when(k == 0)
    def _():
        acc[...] = term

    @pl.when(k > 0)
    def _():
        acc[...] += term

    @pl.when(k == pl.num_programs(0) - 1)
    def _():
        rows = outs[0].shape[0]
        for d, o in enumerate(outs):
            o[...] = acc[d * rows : (d + 1) * rows, :].astype(BF16)


def project(chunks, weight, rows=128, zs=4):
    groups, halves, cores, depth, part, half = weight.shape
    step, inside = cores * zs * part, depth // zs
    steps = groups * inside
    inside_chunk = steps // CHUNKS
    blocks = [b for blocks in chunks for b in blocks]
    tokens = sum(b.shape[0] * b.shape[1] for b in chunks[0])
    devices, cols = tokens // rows, halves * half

    def block_spec(c, b):
        return pl.BlockSpec(
            b.shape[:2] + (step,), lambda k: (0, 0, jnp.clip(k - c * inside_chunk, 0, inside_chunk - 1))
        )

    return pl.pallas_call(
        functools.partial(project_kernel, inside_chunk, len(blocks)),
        grid=(steps,),
        in_specs=[block_spec(c, b) for c, blocks in enumerate(chunks) for b in blocks]
        + [pl.BlockSpec((1, halves, cores, zs, part, half), lambda k: (k // inside, 0, 0, k % inside, 0, 0))],
        out_specs=[pl.BlockSpec((rows, cols), lambda k: (0, 0))] * devices,
        out_shape=[jax.ShapeDtypeStruct((rows, cols), BF16)] * devices,
        scratch_shapes=[pltpu.VMEM((tokens, cols), F32), pltpu.VMEM((tokens, step), BF16)],
        compiler_params=params(),
        cost_estimate=pl.CostEstimate(
            flops=2 * tokens * step * steps * cols, bytes_accessed=2 * step * steps * cols, transcendentals=0
        ),
        name="project",
    )(*blocks, in_hbm(weight))


def finish_kernel(x_ref, hidden, gate, p0, p1, p2, p3, out):
    cols = p0.shape[-1] // 2
    for d, p in enumerate((p0, p1, p2, p3)):
        x = lax.rem(x_ref[0] + d, 4)
        for n in range(2):
            where = pl.ds(pl.multiple_of((n * 4 + x) * cols, HEAD), cols)
            term = gate[:, where] * p[:, n * cols : (n + 1) * cols].astype(F32)
            out[:, where] = (hidden[:, where].astype(F32) + term).astype(BF16)


def finish(x, hidden, gate, pieces, blocks=4):
    rows, width = hidden.shape
    step = rows // blocks
    row_spec = pl.BlockSpec((step, width), lambda i, *_: (i, 0))
    return pl.pallas_call(
        finish_kernel,
        grid_spec=pltpu.PrefetchScalarGridSpec(
            num_scalar_prefetch=1,
            grid=(blocks,),
            in_specs=[row_spec, pl.BlockSpec((1, width), lambda i, *_: (0, 0))]
            + [pl.BlockSpec((step, pieces[0].shape[1]), lambda i, *_: (i, 0))] * 4,
            out_specs=row_spec,
        ),
        out_shape=jax.ShapeDtypeStruct(hidden.shape, BF16),
        compiler_params=params(),
        name="finish",
    )(x, hidden, gate[None], *pieces)


def shards(hidden_in, queries, keys, values, query_gain, key_gain, reach_time, reach_rows, reach_cols, out_weight, gate):
    frames, rows, nw, inner = queries.shape
    width = hidden_in.shape[3]
    weight = lax.all_gather(out_weight, "z", axis=0, tiled=False)
    tokens = [a.reshape(frames * rows, nw, inner) for a in (queries, keys, values)]
    qn, r0, r1, *own = prepare(*tokens, query_gain, key_gain)
    masks = mask_tables(
        lax.axis_index(TM) * frames,
        lax.axis_index(SP) * rows,
        frames * axis_size(TM),
        rows * axis_size(SP),
        nw,
    )
    combo = reach_time * 6 + reach_rows * 3 + reach_cols
    heads = reach_time.shape[0] // CHUNKS
    rb, ra = passed_along(r1, SP, 1), passed_along(r0, SP, -1)
    mine, near, a = [], [], None
    halos = [(passed_along(f1, TM, 1), passed_along(f0, TM, -1)) for f0, f1 in zip(own[::2], own[1::2])]
    for c in range(CHUNKS):
        f0, f1 = own[2 * c : 2 * c + 2]
        hb, ha = halos[c]
        corner_b, corner_a = hb, ha
        if c:
            corner_b, corner_a, a = lax.optimization_barrier((hb, ha, a))
            mine[-1] = a
        to_above = jnp.stack([corner_b[1], corner_a[1]])
        if c == 0:
            to_above, rb, ra, weight, halos[1] = lax.optimization_barrier((to_above, rb, ra, weight, halos[1]))
            weight = lax.all_gather(weight, ("y_hi", "y_lo", "core"), axis=0, tiled=False)
            weight = weight.reshape((2, 2, 2) + weight.shape[1:])
        cb = passed_along(to_above, SP, 1)
        ca = passed_along(jnp.stack([corner_b[0], corner_a[0]]), SP, -1)
        a = attend(
            combo[c * heads : (c + 1) * heads], c, qn, (f0, f1), (hb, ha), (rb, ra), (cb, ca), masks
        )
        mine.append(a)
    for a in mine:
        left, right = shifted(a, "x", 1), shifted(a, "x", -1)
        far0, far1 = shifted(left[:1], "x", 1), shifted(right[1:], "x", -1)
        near.append([far0, far1, left, right])
    far, near_left, near_right = project(near, weight)
    mine[0], far = lax.optimization_barrier((mine[0], far))
    (mine,) = project([[a] for a in mine], weight)
    pieces = [mine, shifted(near_left, "x", -1), shifted(far, "x", 2), shifted(near_right, "x", 1)]
    x = lax.axis_index("x").astype(jnp.int32)[None]
    out = finish(x, hidden_in.reshape(-1, width), gate, pieces)
    return out.reshape(hidden_in.shape)


def solution(mesh):
    inner_mesh = Mesh(mesh.devices.reshape(2, 4, 2, 8, 2), TM + SP)
    tokens = P(TM, SP, None, None)
    in_specs = (tokens,) * 4 + (P(),) * 5 + (P(SP, TM), P())
    return jax.shard_map(shards, mesh=inner_mesh, in_specs=in_specs, out_specs=tokens, check_vma=False)
```

```python
import functools

import jax
import jax.numpy as jnp
from jax import lax
from jax.experimental import pallas as pl
from jax.experimental.pallas import tpu as pltpu
from jax.sharding import Mesh, PartitionSpec as P

TW = 8
HEAD = 128
TM = ("y_lo", "x")
SP = ("y_hi", "z", "core")
COMBOS = 12
F32, BF16 = jnp.float32, jnp.bfloat16


def axis_size(axes):
    n = 1
    for a in axes:
        n *= lax.axis_size(a)
    return n


def passed_along(block, axes, distance):
    n = axis_size(axes)
    route = [(i - distance, i) for i in range(n) if 0 <= i - distance < n]
    return lax.ppermute(block, axes, route)


def along_y(block, target):
    at = lambda y: (y % 2) * 2 + y // 2
    return lax.ppermute(block, ("y_lo", "y_hi"), [(at(y), at(target(y))) for y in range(4)])


def in_hbm(array):
    return pltpu.with_memory_space_constraint(array, pltpu.HBM)


def params(megabytes=24):
    return pltpu.CompilerParams(vmem_limit_bytes=megabytes << 20)


def prepare_kernel(q_ref, k_ref, v_ref, qg_ref, kg_ref, qn_ref, *outs):
    i = pl.program_id(0)
    f, r = i // 2, i % 2
    inner = q_ref.shape[-1]

    def normed(ref, gain):
        a = ref[0].astype(F32)
        ms = jnp.sum(a * a, axis=-1, keepdims=True) * (1.0 / inner)
        return (a * lax.rsqrt(ms + 1e-06) * gain[...]).astype(BF16)

    qn_ref[0] = normed(q_ref, qg_ref)
    kn = normed(k_ref, kg_ref)
    v = v_ref[0]
    f0, f1, r0, r1 = outs
    for chosen, ref in ((f == 0, f0), (f == 1, f1), (r == 0, r0), (r == 1, r1)):

        @pl.when(chosen)
        def _(ref=ref):
            ref[0, 0] = kn
            ref[0, 1] = v


def prepare(queries, keys, values, query_gain, key_gain):
    groups, nw, inner = queries.shape
    token_spec = pl.BlockSpec((1, nw, inner), lambda i: (i, 0, 0))
    gain_spec = pl.BlockSpec((1, inner), lambda i: (0, 0))
    out_shape = [pltpu.HBM(queries.shape, BF16)]
    out_specs = [token_spec]
    out_shape += [pltpu.HBM((2, 2, nw, inner), BF16)] * 4
    out_specs += [
        pl.BlockSpec((1, 2, nw, inner), lambda i: (jnp.minimum(i, 1), 0, 0, 0)),
            pl.BlockSpec((1, 2, nw, inner), lambda i: (jnp.maximum(i - 2, 0), 0, 0, 0)),
            pl.BlockSpec((1, 2, nw, inner), lambda i: (i // 2, 0, 0, 0)),
            pl.BlockSpec((1, 2, nw, inner), lambda i: (i // 2, 0, 0, 0)),
        ]
    return pl.pallas_call(
        prepare_kernel,
        grid=(groups,),
        in_specs=[token_spec] * 3 + [gain_spec] * 2,
        out_specs=out_specs,
        out_shape=out_shape,
        compiler_params=params(),
        cost_estimate=pl.CostEstimate(flops=0, bytes_accessed=12 << 20, transcendentals=0),
        name="prepare",
    )(*[in_hbm(a) for a in (queries, keys, values)], query_gain[None], key_gain[None])


def mask_tables(first_frame, first_row, frame_count, row_count, nw):
    i32 = jnp.int32
    shape = (COMBOS, 2, 2 * nw, 3 * 4 * nw)
    t = lax.broadcasted_iota(i32, shape, 0)
    f = lax.broadcasted_iota(i32, shape, 1)
    q = lax.broadcasted_iota(i32, shape, 2)
    k = lax.broadcasted_iota(i32, shape, 3)
    kf, kr, kc = k // (4 * nw), k // nw % 4, k % nw
    frame, row = first_frame - 1 + f + kf, first_row - 1 + kr
    allowed = jnp.abs(kf - 1) <= t // 6
    allowed &= jnp.abs(q // nw + 1 - kr) <= t // 3 % 2
    allowed &= jnp.abs(q % nw // TW - kc // TW) <= t % 3
    allowed &= (frame >= 0) & (frame < frame_count) & (row >= 0) & (row < row_count)
    return jnp.where(allowed, 0.0, -jnp.inf).astype(F32)


def attend_kernel(heads, scale, combo_ref, half_ref, q_ref, f0, f1, hb, ha, rb, ra, cb, ca, mask_ref, same_ref, other_ref):
    step = pl.program_id(0)
    frames = ((cb.at[0], hb, ca.at[0]), (rb.at[0], f0, ra.at[0]), (rb.at[1], f1, ra.at[1]), (cb.at[1], ha, ca.at[1]))

    def region(kv, lanes):
        parts = []
        for below, own, above in frames:
            parts += [below[kv, :, lanes], own[0, kv, :, lanes], own[1, kv, :, lanes], above[kv, :, lanes]]
        return jnp.concatenate(parts, axis=0)

    scores = {}
    for h in range(heads):
        lanes = slice(h * HEAD, (h + 1) * HEAD)
        keys = region(0, lanes)
        group = keys.shape[0] // 4
        combo = combo_ref[step * heads + h]
        for f in range(2):
            q = q_ref[2 * f : 2 * f + 2, :, lanes].reshape(-1, HEAD)
            k = keys[f * group : (f + 3) * group]
            s = lax.dot_general(q, k, (((1,), (1,)), ((), ())), preferred_element_type=F32)
            scores[h, f] = s + mask_ref[combo, f]
    weights = {}
    for at, s in scores.items():
        peak = jnp.max(s, axis=1, keepdims=True)
        w = jnp.exp((s - peak) * scale)
        weights[at] = w.astype(BF16), jnp.sum(w, axis=1, keepdims=True)
    mixed = {}
    for h in range(heads):
        lanes = slice(h * HEAD, (h + 1) * HEAD)
        values = region(1, lanes)
        group = values.shape[0] // 4
        for f in range(2):
            w, total = weights[h, f]
            o = jnp.dot(w, values[f * group : (f + 3) * group], preferred_element_type=F32)
            mixed[h, f] = (o / total).astype(BF16)
    in_half = step // (pl.num_programs(0) // 2) == half_ref[0]
    for chosen, ref in ((in_half, same_ref), (jnp.logical_not(in_half), other_ref)):

        @pl.when(chosen)
        def _(ref=ref):
            for (h, f), o in mixed.items():
                ref[f * o.shape[0] : (f + 1) * o.shape[0], h * HEAD : (h + 1) * HEAD] = o


def attend(combo, half, qn, own, halos, masks, heads=10):
    groups, nw, inner = qn.shape
    lanes = heads * HEAD
    steps = inner // lanes
    inside = steps // 2
    kv_spec = pl.BlockSpec((2, 2, nw, lanes), lambda i, *_: (0, 0, 0, i))
    same = lambda i, _, half_ref: (0, jnp.clip(i - inside * half_ref[0], 0, inside - 1))
    other = lambda i, _, half_ref: (0, jnp.clip(i - inside * (1 - half_ref[0]), 0, inside - 1))
    return pl.pallas_call(
        functools.partial(attend_kernel, heads, HEAD**-0.5),
        grid_spec=pltpu.PrefetchScalarGridSpec(
            num_scalar_prefetch=2,
            grid=(steps,),
            in_specs=[pl.BlockSpec((groups, nw, lanes), lambda i, *_: (0, 0, i))]
            + [kv_spec] * 8
            + [pl.BlockSpec(masks.shape, lambda i, *_: (0, 0, 0, 0))],
            out_specs=[pl.BlockSpec((groups * nw, lanes), same), pl.BlockSpec((groups * nw, lanes), other)],
        ),
        out_shape=[pltpu.HBM((groups * nw, inner // 2), BF16)] * 2,
        compiler_params=params(),
        cost_estimate=pl.CostEstimate(flops=4 * 128 * 384 * inner, bytes_accessed=32 << 20, transcendentals=0),
        name="attend",
    )(combo, half, qn, *own, *halos, masks)


def project_kernel(blocks, *refs):
    ins, w_ref, outs, a_buf = refs[:blocks], refs[blocks], refs[blocks + 1 : -1], refs[-1]

    @pl.when(pl.program_id(0) == 0)
    def _():
        a_buf[...] = jnp.concatenate([i[...] for i in ins], axis=0)

    _, cores, zs, _, _ = w_ref.shape
    w = jnp.concatenate([w_ref[0, c, z] for z in range(zs) for c in range(cores)], axis=0)
    term = jnp.dot(a_buf[...], w, preferred_element_type=F32)
    rows = outs[0].shape[0]
    for d, o in enumerate(outs):
        o[...] = term[d * rows : (d + 1) * rows, :].astype(BF16)


def project(blocks, weight):
    rows, depth = blocks[0].shape
    xs, cores, zs, part, cols = weight.shape
    return pl.pallas_call(
        functools.partial(project_kernel, len(blocks)),
        grid=(xs,),
        in_specs=[pl.BlockSpec((rows, depth), lambda j: (0, 0))] * len(blocks)
        + [pl.BlockSpec((1, cores, zs, part, cols), lambda j: (j, 0, 0, 0, 0))],
        out_specs=[pl.BlockSpec((rows, cols), lambda j: (0, j))] * len(blocks),
        out_shape=[jax.ShapeDtypeStruct((rows, xs * cols), BF16)] * len(blocks),
        scratch_shapes=[pltpu.VMEM((len(blocks) * rows, depth), BF16)],
        compiler_params=params(32),
        cost_estimate=pl.CostEstimate(
            flops=2 * len(blocks) * rows * depth * xs * cols, bytes_accessed=2 * depth * xs * cols, transcendentals=0
        ),
        name="project",
    )(*blocks, in_hbm(weight))


def finish_kernel(y_ref, hidden, gate, same0, same1, other0, other1, out):
    half = same0.shape[-1]
    for side, (p, q) in ((y_ref[0], (same0, same1)), (1 - y_ref[0], (other0, other1))):
        where = pl.ds(pl.multiple_of(side * half, HEAD), half)
        branch = p[...].astype(F32) + q[...].astype(F32)
        out[:, where] = (hidden[:, where].astype(F32) + gate[:, where] * branch).astype(BF16)


def finish(y_lo, hidden, gate, pieces, blocks=4):
    rows, width = hidden.shape
    step = rows // blocks
    row_spec = pl.BlockSpec((step, width), lambda i, *_: (i, 0))
    return pl.pallas_call(
        finish_kernel,
        grid_spec=pltpu.PrefetchScalarGridSpec(
            num_scalar_prefetch=1,
            grid=(blocks,),
            in_specs=[row_spec, pl.BlockSpec((1, width), lambda i, *_: (0, 0))]
            + [pl.BlockSpec((step, pieces[0].shape[1]), lambda i, *_: (i, 0))] * 4,
            out_specs=row_spec,
        ),
        out_shape=jax.ShapeDtypeStruct(hidden.shape, BF16),
        compiler_params=params(),
        name="finish",
    )(y_lo, hidden, gate[None], *pieces)


def shards(hidden_in, queries, keys, values, query_gain, key_gain, reach_time, reach_rows, reach_cols, out_weight, gate):
    frames, rows, nw, inner = queries.shape
    width = hidden_in.shape[3]
    weight = lax.all_gather(out_weight, "z", axis=0, tiled=False)
    tokens = [a.reshape(frames * rows, nw, inner) for a in (queries, keys, values)]
    qn, *own = prepare(*tokens, query_gain, key_gain)
    masks = mask_tables(
        lax.axis_index(TM) * frames,
        lax.axis_index(SP) * rows,
        frames * axis_size(TM),
        rows * axis_size(SP),
        nw,
    )
    combo = reach_time * 6 + reach_rows * 3 + reach_cols
    f0, f1, r0, r1 = own
    hb, ha = passed_along(f1, TM, 1), passed_along(f0, TM, -1)
    rb, ra = passed_along(r1, SP, 1), passed_along(r0, SP, -1)
    cb = passed_along(jnp.stack([hb[1], ha[1]]), SP, 1)
    ca = passed_along(jnp.stack([hb[0], ha[0]]), SP, -1)
    hb_in, ha_in, rb, ra, weight = lax.optimization_barrier((hb, ha, rb, ra, weight))
    weight = lax.all_gather(weight, ("x", "core"), axis=0, tiled=False)
    weight = weight.reshape((lax.axis_size("x"), lax.axis_size("core")) + weight.shape[1:])
    y_hi, y_lo = (lax.axis_index(a).astype(jnp.int32)[None] for a in ("y_hi", "y_lo"))
    same, other = attend(combo, y_hi, qn, (f0, f1), (hb_in, ha_in, rb, ra, cb, ca), masks)
    pair = [along_y(same, lambda y: y ^ 1), along_y(other, lambda y: 3 - y), along_y(other, lambda y: y ^ 2)]
    to_pair, to_across, to_far = project(pair, weight)
    same, to_far = lax.optimization_barrier((same, to_far))
    (mine,) = project([same], weight)
    far = along_y(to_far, lambda y: y ^ 2)
    pieces = [mine, far, along_y(to_pair, lambda y: y ^ 1), along_y(to_across, lambda y: 3 - y)]
    out = finish(y_lo, hidden_in.reshape(-1, width), gate, pieces)
    return out.reshape(hidden_in.shape)


def solution(mesh):
    inner_mesh = Mesh(mesh.devices.reshape(2, 4, 2, 8, 2), TM + SP)
    tokens = P(TM, SP, None, None)
    in_specs = (tokens,) * 4 + (P(),) * 5 + (P(SP, TM), P())
    return jax.shard_map(shards, mesh=inner_mesh, in_specs=in_specs, out_specs=tokens, check_vma=False)
```

```python
import functools

import jax
import jax.numpy as jnp
from jax import lax
from jax.experimental import pallas as pl
from jax.experimental.pallas import tpu as pltpu
from jax.sharding import Mesh, PartitionSpec as P

TW = 8
HEAD = 128
TM = ("y_lo", "x")
SP = ("y_hi", "z", "core")
COMBOS = 12
F32, BF16 = jnp.float32, jnp.bfloat16


def axis_size(axes):
    n = 1
    for a in axes:
        n *= lax.axis_size(a)
    return n


def passed_along(block, axes, distance):
    n = axis_size(axes)
    route = [(i - distance, i) for i in range(n) if 0 <= i - distance < n]
    return lax.ppermute(block, axes, route)


def shifted(block, axis, distance):
    n = lax.axis_size(axis)
    return lax.ppermute(block, axis, [(i, (i + distance) % n) for i in range(n)])


def in_hbm(array):
    return pltpu.with_memory_space_constraint(array, pltpu.HBM)


def params(megabytes=24):
    return pltpu.CompilerParams(vmem_limit_bytes=megabytes << 20)


def prepare_kernel(q_ref, k_ref, qg_ref, kg_ref, qn_ref, *outs):
    i = pl.program_id(0)
    f, r = i // 2, i % 2
    inner = q_ref.shape[-1]

    def normed(ref, gain):
        a = ref[0].astype(F32)
        ms = jnp.sum(a * a, axis=-1, keepdims=True) * (1.0 / inner)
        return (a * lax.rsqrt(ms + 1e-06) * gain[...]).astype(BF16)

    qn_ref[0] = normed(q_ref, qg_ref)
    kn = normed(k_ref, kg_ref)
    f0, f1, r0, r1 = outs
    for chosen, ref in ((f == 0, f0), (f == 1, f1), (r == 0, r0), (r == 1, r1)):

        @pl.when(chosen)
        def _(ref=ref):
            ref[0] = kn


def prepare(queries, keys, query_gain, key_gain):
    groups, nw, inner = queries.shape
    token_spec = pl.BlockSpec((1, nw, inner), lambda i: (i, 0, 0))
    gain_spec = pl.BlockSpec((1, inner), lambda i: (0, 0))
    out_shape = [pltpu.HBM(queries.shape, BF16)]
    out_shape += [pltpu.HBM((2, nw, inner), BF16)] * 4
    out_specs = [
        token_spec,
        pl.BlockSpec((1, nw, inner), lambda i: (jnp.minimum(i, 1), 0, 0)),
        pl.BlockSpec((1, nw, inner), lambda i: (jnp.maximum(i - 2, 0), 0, 0)),
        pl.BlockSpec((1, nw, inner), lambda i: (i // 2, 0, 0)),
        pl.BlockSpec((1, nw, inner), lambda i: (i // 2, 0, 0)),
    ]
    return pl.pallas_call(
        prepare_kernel,
        grid=(groups,),
        in_specs=[token_spec] * 2 + [gain_spec] * 2,
        out_specs=out_specs,
        out_shape=out_shape,
        compiler_params=params(),
        cost_estimate=pl.CostEstimate(flops=0, bytes_accessed=12 << 20, transcendentals=0),
        name="prepare",
    )(in_hbm(queries), in_hbm(keys), query_gain[None], key_gain[None])


def mask_tables(first_frame, first_row, frame_count, row_count, nw):
    i32 = jnp.int32
    shape = (COMBOS, 2, 2 * nw, 3 * 4 * nw)
    t = lax.broadcasted_iota(i32, shape, 0)
    f = lax.broadcasted_iota(i32, shape, 1)
    q = lax.broadcasted_iota(i32, shape, 2)
    k = lax.broadcasted_iota(i32, shape, 3)
    kf, kr, kc = k // (4 * nw), k // nw % 4, k % nw
    frame, row = first_frame - 1 + f + kf, first_row - 1 + kr
    allowed = jnp.abs(kf - 1) <= t // 6
    allowed &= jnp.abs(q // nw + 1 - kr) <= t // 3 % 2
    allowed &= jnp.abs(q % nw // TW - kc // TW) <= t % 3
    allowed &= (frame >= 0) & (frame < frame_count) & (row >= 0) & (row < row_count)
    return jnp.where(allowed, 0.0, -jnp.inf).astype(F32)


def attend_kernel(
    heads, scale, combo_ref, q_ref, k0, k1, v_ref, kb, ka, vb, va, rkb, rka, rvb, rva, cb, ca, mask_ref, *out_refs
):
    step = pl.program_id(0)
    keys_by_frame, values_by_frame = (kb, k0, k1, ka), (vb, v_ref.at[:2], v_ref.at[2:], va)
    rows = ((rkb, rka), (rvb, rva))

    def region(kv, lanes):
        parts = []
        for frame, own in enumerate((keys_by_frame, values_by_frame)[kv]):
            if frame in (0, 3):
                below, above = (ref[frame // 3, kv, :, lanes] for ref in (cb, ca))
            else:
                below, above = (ref[frame - 1, :, lanes] for ref in rows[kv])
            parts += [below, own[0, :, lanes], own[1, :, lanes], above]
        return jnp.concatenate(parts, axis=0)

    scores = {}
    for h in range(heads):
        lanes = slice(h * HEAD, (h + 1) * HEAD)
        keys = region(0, lanes)
        group = keys.shape[0] // 4
        combo = combo_ref[step * heads + h]
        for f in range(2):
            q = q_ref[2 * f : 2 * f + 2, :, lanes].reshape(-1, HEAD)
            k = keys[f * group : (f + 3) * group]
            s = lax.dot_general(q, k, (((1,), (1,)), ((), ())), preferred_element_type=F32)
            scores[h, f] = s + mask_ref[combo, f]
    weights = {}
    for at, s in scores.items():
        peak = jnp.max(s, axis=1, keepdims=True)
        w = jnp.exp((s - peak) * scale)
        weights[at] = w.astype(BF16), jnp.sum(w, axis=1, keepdims=True)
    for h in range(heads):
        lanes = slice(h * HEAD, (h + 1) * HEAD)
        values = region(1, lanes)
        group = values.shape[0] // 4
        for f in range(2):
            w, total = weights[h, f]
            o = jnp.dot(w, values[f * group : (f + 3) * group], preferred_element_type=F32)
            out_refs[f][:, lanes] = (o / total).astype(BF16)


def attend(combo, qn, keys, values, halos, corners, masks, heads=8):
    groups, nw, inner = qn.shape
    lanes = heads * HEAD
    token_spec = pl.BlockSpec((groups, nw, lanes), lambda i, *_: (0, 0, i))
    frame_spec = pl.BlockSpec((2, nw, lanes), lambda i, *_: (0, 0, i))
    corner_spec = pl.BlockSpec((2, 2, nw, lanes), lambda i, *_: (0, 0, 0, i))
    return pl.pallas_call(
        functools.partial(attend_kernel, heads, HEAD**-0.5),
        grid_spec=pltpu.PrefetchScalarGridSpec(
            num_scalar_prefetch=1,
            grid=(inner // lanes,),
            in_specs=[token_spec]
            + [frame_spec] * 2
            + [token_spec]
            + [frame_spec] * 8
            + [corner_spec] * 2
            + [pl.BlockSpec(masks.shape, lambda i, *_: (0, 0, 0, 0))],
            out_specs=[pl.BlockSpec((2 * nw, lanes), lambda i, *_: (0, i))] * 2,
        ),
        out_shape=[pltpu.HBM((2 * nw, inner), BF16)] * 2,
        compiler_params=params(),
        cost_estimate=pl.CostEstimate(flops=4 * 128 * 384 * inner, bytes_accessed=32 << 20, transcendentals=0),
        name="attend",
    )(combo, qn, *keys, values, *halos, *corners, masks)


def project_kernel(blocks, *refs):
    ins, w_ref, outs, acc = refs[:blocks], refs[blocks], refs[blocks + 1 : -1], refs[-1]
    k = pl.program_id(0)
    a = jnp.concatenate([i[...] for i in ins], axis=0)
    _, halves, cores, zs, _, _ = w_ref.shape
    w = jnp.concatenate(
        [
            jnp.concatenate([w_ref[0, n, c, z] for z in range(zs) for c in range(cores)], axis=0)
            for n in range(halves)
        ],
        axis=1,
    )
    term = jnp.dot(a, w, preferred_element_type=F32)

    @pl.when(k == 0)
    def _():
        acc[...] = term

    @pl.when(k > 0)
    def _():
        acc[...] += term

    @pl.when(k == pl.num_programs(0) - 1)
    def _():
        rows = outs[0].shape[0]
        for d, o in enumerate(outs):
            o[...] = acc[d * rows : (d + 1) * rows, :].astype(BF16)


def project(blocks, weight, zs=4):
    rows, inner = blocks[0].shape
    groups, halves, cores, depth, part, half = weight.shape
    cols, devices, inside, step = halves * half, len(blocks) // 2, depth // zs, cores * zs * part
    return pl.pallas_call(
        functools.partial(project_kernel, len(blocks)),
        grid=(groups * inside,),
        in_specs=[pl.BlockSpec((rows, step), lambda k: (0, k))] * len(blocks)
        + [pl.BlockSpec((1, halves, cores, zs, part, half), lambda k: (k // inside, 0, 0, k % inside, 0, 0))],
        out_specs=[pl.BlockSpec((2 * rows, cols), lambda k: (0, 0))] * devices,
        out_shape=[jax.ShapeDtypeStruct((2 * rows, cols), BF16)] * devices,
        scratch_shapes=[pltpu.VMEM((2 * devices * rows, cols), F32)],
        compiler_params=params(40),
        cost_estimate=pl.CostEstimate(
            flops=4 * devices * rows * inner * cols, bytes_accessed=2 * inner * cols, transcendentals=0
        ),
        name="project",
    )(*blocks, in_hbm(weight))


def finish_kernel(x_ref, hidden, gate, p0, p1, p2, p3, out):
    cols = p0.shape[-1] // 2
    for d, p in enumerate((p0, p1, p2, p3)):
        x = lax.rem(x_ref[0] + d, 4)
        for n in range(2):
            where = pl.ds(pl.multiple_of((n * 4 + x) * cols, HEAD), cols)
            term = gate[:, where] * p[:, n * cols : (n + 1) * cols].astype(F32)
            out[:, where] = (hidden[:, where].astype(F32) + term).astype(BF16)


def finish(x, hidden, gate, pieces, blocks=4):
    rows, width = hidden.shape
    step = rows // blocks
    row_spec = pl.BlockSpec((step, width), lambda i, *_: (i, 0))
    return pl.pallas_call(
        finish_kernel,
        grid_spec=pltpu.PrefetchScalarGridSpec(
            num_scalar_prefetch=1,
            grid=(blocks,),
            in_specs=[row_spec, pl.BlockSpec((1, width), lambda i, *_: (0, 0))]
            + [pl.BlockSpec((step, pieces[0].shape[1]), lambda i, *_: (i, 0))] * 4,
            out_specs=row_spec,
        ),
        out_shape=jax.ShapeDtypeStruct(hidden.shape, BF16),
        compiler_params=params(),
        name="finish",
    )(x, hidden, gate[None], *pieces)


def shards(hidden_in, queries, keys, values, query_gain, key_gain, reach_time, reach_rows, reach_cols, out_weight, gate):
    frames, rows, nw, inner = queries.shape
    width = hidden_in.shape[3]
    weight = lax.all_gather(out_weight, "z", axis=0, tiled=False)
    vb, va = passed_along(values[1], TM, 1), passed_along(values[0], TM, -1)
    rvb, rva = passed_along(values[:, 1], SP, 1), passed_along(values[:, 0], SP, -1)

    q_tokens, k_tokens, v_tokens = [a.reshape(frames * rows, nw, inner) for a in (queries, keys, values)]
    qn, k0, k1, kr0, kr1 = prepare(q_tokens, k_tokens, query_gain, key_gain)
    masks = mask_tables(
        lax.axis_index(TM) * frames,
        lax.axis_index(SP) * rows,
        frames * axis_size(TM),
        rows * axis_size(SP),
        nw,
    )
    combo = reach_time * 6 + reach_rows * 3 + reach_cols
    sent = lax.optimization_barrier((k0, k1, kr0, kr1, vb, va, rvb, rva))
    k0, k1, kr0, kr1, vb, va, rvb, rva = sent
    kb, ka = passed_along(k1, TM, 1), passed_along(k0, TM, -1)
    rkb, rka = passed_along(kr1, SP, 1), passed_along(kr0, SP, -1)
    halos = kb, ka, vb, va, rkb, rka, rvb, rva
    *halos, weight = lax.optimization_barrier((*halos, weight))
    kb, ka, vb, va = halos[:4]
    weight = lax.all_gather(weight, ("y_hi", "y_lo", "core"), axis=0, tiled=False)
    weight = weight.reshape((2, 2, 2) + weight.shape[1:])
    cb = passed_along(jnp.stack([jnp.stack([kb[1], vb[1]]), jnp.stack([ka[1], va[1]])]), SP, 1)
    ca = passed_along(jnp.stack([jnp.stack([kb[0], vb[0]]), jnp.stack([ka[0], va[0]])]), SP, -1)
    a0, a1 = attend(combo, qn, (k0, k1), v_tokens, halos, (cb, ca), masks)
    left0, right1 = shifted(a0, "x", 1), shifted(a1, "x", -1)
    left1, right0 = shifted(a1, "x", 1), shifted(a0, "x", -1)
    far0, far1 = shifted(left0, "x", 1), shifted(right1, "x", -1)
    far, near_left, near_right = project([far0, far1, left0, left1, right0, right1], weight)
    a0, far = lax.optimization_barrier((a0, far))
    (mine,) = project([a0, a1], weight)
    pieces = [mine, shifted(near_left, "x", -1), shifted(far, "x", 2), shifted(near_right, "x", 1)]
    x = lax.axis_index("x").astype(jnp.int32)[None]
    out = finish(x, hidden_in.reshape(-1, width), gate, pieces)
    return out.reshape(hidden_in.shape)


def solution(mesh):
    inner_mesh = Mesh(mesh.devices.reshape(2, 4, 2, 8, 2), TM + SP)
    tokens = P(TM, SP, None, None)
    in_specs = (tokens,) * 4 + (P(),) * 5 + (P(SP, TM), P())
    return jax.shard_map(shards, mesh=inner_mesh, in_specs=in_specs, out_specs=tokens, check_vma=False)
```

```python
import functools

import jax
import jax.numpy as jnp
from jax import lax
from jax.experimental import pallas as pl
from jax.experimental.pallas import tpu as pltpu
from jax.sharding import Mesh, PartitionSpec as P

TW = 8
HEAD = 128
TM = ("y_lo", "x")
SP = ("y_hi", "z", "core")
COMBOS = 12
F32, BF16 = jnp.float32, jnp.bfloat16


def axis_size(axes):
    n = 1
    for a in axes:
        n *= lax.axis_size(a)
    return n


def passed_along(block, axes, distance):
    n = axis_size(axes)
    route = [(i - distance, i) for i in range(n) if 0 <= i - distance < n]
    return lax.ppermute(block, axes, route)


def along_y(block, target):
    at = lambda y: (y % 2) * 2 + y // 2
    return lax.ppermute(block, ("y_lo", "y_hi"), [(at(y), at(target(y))) for y in range(4)])


def in_hbm(array):
    return pltpu.with_memory_space_constraint(array, pltpu.HBM)


def params(megabytes=24):
    return pltpu.CompilerParams(vmem_limit_bytes=megabytes << 20)


def prepare_kernel(q_ref, k_ref, v_ref, qg_ref, kg_ref, qn_ref, *outs):
    i = pl.program_id(0)
    f, r = i // 2, i % 2
    inner = q_ref.shape[-1]

    def normed(ref, gain):
        a = ref[0].astype(F32)
        ms = jnp.sum(a * a, axis=-1, keepdims=True) * (1.0 / inner)
        return (a * lax.rsqrt(ms + 1e-06) * gain[...]).astype(BF16)

    qn_ref[0] = normed(q_ref, qg_ref)
    kn = normed(k_ref, kg_ref)
    v = v_ref[0]
    f0, f1, r0, r1 = outs
    for chosen, ref in ((f == 0, f0), (f == 1, f1), (r == 0, r0), (r == 1, r1)):

        @pl.when(chosen)
        def _(ref=ref):
            ref[0, 0] = kn
            ref[0, 1] = v


def prepare(queries, keys, values, query_gain, key_gain):
    groups, nw, inner = queries.shape
    token_spec = pl.BlockSpec((1, nw, inner), lambda i: (i, 0, 0))
    gain_spec = pl.BlockSpec((1, inner), lambda i: (0, 0))
    out_shape = [pltpu.HBM(queries.shape, BF16)]
    out_specs = [token_spec]
    out_shape += [pltpu.HBM((2, 2, nw, inner), BF16)] * 4
    out_specs += [
        pl.BlockSpec((1, 2, nw, inner), lambda i: (jnp.minimum(i, 1), 0, 0, 0)),
            pl.BlockSpec((1, 2, nw, inner), lambda i: (jnp.maximum(i - 2, 0), 0, 0, 0)),
            pl.BlockSpec((1, 2, nw, inner), lambda i: (i // 2, 0, 0, 0)),
            pl.BlockSpec((1, 2, nw, inner), lambda i: (i // 2, 0, 0, 0)),
        ]
    return pl.pallas_call(
        prepare_kernel,
        grid=(groups,),
        in_specs=[token_spec] * 3 + [gain_spec] * 2,
        out_specs=out_specs,
        out_shape=out_shape,
        compiler_params=params(),
        cost_estimate=pl.CostEstimate(flops=0, bytes_accessed=12 << 20, transcendentals=0),
        name="prepare",
    )(*[in_hbm(a) for a in (queries, keys, values)], query_gain[None], key_gain[None])


def mask_tables(first_frame, first_row, frame_count, row_count, nw):
    i32 = jnp.int32
    shape = (COMBOS, 2, 2 * nw, 3 * 4 * nw)
    t = lax.broadcasted_iota(i32, shape, 0)
    f = lax.broadcasted_iota(i32, shape, 1)
    q = lax.broadcasted_iota(i32, shape, 2)
    k = lax.broadcasted_iota(i32, shape, 3)
    kf, kr, kc = k // (4 * nw), k // nw % 4, k % nw
    frame, row = first_frame - 1 + f + kf, first_row - 1 + kr
    allowed = jnp.abs(kf - 1) <= t // 6
    allowed &= jnp.abs(q // nw + 1 - kr) <= t // 3 % 2
    allowed &= jnp.abs(q % nw // TW - kc // TW) <= t % 3
    allowed &= (frame >= 0) & (frame < frame_count) & (row >= 0) & (row < row_count)
    return jnp.where(allowed, 0.0, -jnp.inf).astype(F32)


def attend_kernel(heads, scale, combo_ref, half_ref, q_ref, f0, f1, hb, ha, rb, ra, cb, ca, mask_ref, same_ref, other_ref):
    step = pl.program_id(0)
    frames = ((cb.at[0], hb, ca.at[0]), (rb.at[0], f0, ra.at[0]), (rb.at[1], f1, ra.at[1]), (cb.at[1], ha, ca.at[1]))

    def region(kv, lanes):
        parts = []
        for below, own, above in frames:
            parts += [below[kv, :, lanes], own[0, kv, :, lanes], own[1, kv, :, lanes], above[kv, :, lanes]]
        return jnp.concatenate(parts, axis=0)

    scores = {}
    for h in range(heads):
        lanes = slice(h * HEAD, (h + 1) * HEAD)
        keys = region(0, lanes)
        group = keys.shape[0] // 4
        combo = combo_ref[step * heads + h]
        for f in range(2):
            q = q_ref[2 * f : 2 * f + 2, :, lanes].reshape(-1, HEAD)
            k = keys[f * group : (f + 3) * group]
            s = lax.dot_general(q, k, (((1,), (1,)), ((), ())), preferred_element_type=F32)
            scores[h, f] = s + mask_ref[combo, f]
    weights = {}
    for at, s in scores.items():
        peak = jnp.max(s, axis=1, keepdims=True)
        w = jnp.exp((s - peak) * scale)
        weights[at] = w.astype(BF16), jnp.sum(w, axis=1, keepdims=True)
    mixed = {}
    for h in range(heads):
        lanes = slice(h * HEAD, (h + 1) * HEAD)
        values = region(1, lanes)
        group = values.shape[0] // 4
        for f in range(2):
            w, total = weights[h, f]
            o = jnp.dot(w, values[f * group : (f + 3) * group], preferred_element_type=F32)
            mixed[h, f] = (o / total).astype(BF16)
    in_half = step // (pl.num_programs(0) // 2) == half_ref[0]
    for chosen, ref in ((in_half, same_ref), (jnp.logical_not(in_half), other_ref)):

        @pl.when(chosen)
        def _(ref=ref):
            for (h, f), o in mixed.items():
                ref[f * o.shape[0] : (f + 1) * o.shape[0], h * HEAD : (h + 1) * HEAD] = o


def attend(combo, half, qn, own, halos, masks, heads=10):
    groups, nw, inner = qn.shape
    lanes = heads * HEAD
    steps = inner // lanes
    inside = steps // 2
    kv_spec = pl.BlockSpec((2, 2, nw, lanes), lambda i, *_: (0, 0, 0, i))
    same = lambda i, _, half_ref: (0, jnp.clip(i - inside * half_ref[0], 0, inside - 1))
    other = lambda i, _, half_ref: (0, jnp.clip(i - inside * (1 - half_ref[0]), 0, inside - 1))
    return pl.pallas_call(
        functools.partial(attend_kernel, heads, HEAD**-0.5),
        grid_spec=pltpu.PrefetchScalarGridSpec(
            num_scalar_prefetch=2,
            grid=(steps,),
            in_specs=[pl.BlockSpec((groups, nw, lanes), lambda i, *_: (0, 0, i))]
            + [kv_spec] * 8
            + [pl.BlockSpec(masks.shape, lambda i, *_: (0, 0, 0, 0))],
            out_specs=[pl.BlockSpec((groups * nw, lanes), same), pl.BlockSpec((groups * nw, lanes), other)],
        ),
        out_shape=[pltpu.HBM((groups * nw, inner // 2), BF16)] * 2,
        compiler_params=params(),
        cost_estimate=pl.CostEstimate(flops=4 * 128 * 384 * inner, bytes_accessed=32 << 20, transcendentals=0),
        name="attend",
    )(combo, half, qn, *own, *halos, masks)


def project_kernel(blocks, *refs):
    ins, w_ref, outs, a_buf = refs[:blocks], refs[blocks], refs[blocks + 1 : -1], refs[-1]

    @pl.when(pl.program_id(0) == 0)
    def _():
        a_buf[...] = jnp.concatenate([i[...] for i in ins], axis=0)

    _, cores, zs, _, _ = w_ref.shape
    w = jnp.concatenate([w_ref[0, c, z] for z in range(zs) for c in range(cores)], axis=0)
    term = jnp.dot(a_buf[...], w, preferred_element_type=F32)
    rows = outs[0].shape[0]
    for d, o in enumerate(outs):
        o[...] = term[d * rows : (d + 1) * rows, :].astype(BF16)


def project(blocks, weight, first, count):
    rows, depth = blocks[0].shape
    _, cores, zs, part, cols = weight.shape
    return pl.pallas_call(
        functools.partial(project_kernel, len(blocks)),
        grid=(count,),
        in_specs=[pl.BlockSpec((rows, depth), lambda j: (0, 0))] * len(blocks)
        + [pl.BlockSpec((1, cores, zs, part, cols), lambda j: (first + j, 0, 0, 0, 0))],
        out_specs=[pl.BlockSpec((rows, cols), lambda j: (0, j))] * len(blocks),
        out_shape=[jax.ShapeDtypeStruct((rows, count * cols), BF16)] * len(blocks),
        scratch_shapes=[pltpu.VMEM((len(blocks) * rows, depth), BF16)],
        compiler_params=params(32),
        cost_estimate=pl.CostEstimate(
            flops=2 * len(blocks) * rows * depth * count * cols,
            bytes_accessed=2 * depth * count * cols,
            transcendentals=0,
        ),
        name="project",
    )(*blocks, in_hbm(weight))


def finish_kernel(y_ref, hidden, gate, mine, far0, pair0, across0, far1, pair1, across1, out):
    half, split = mine.shape[-1], far0.shape[-1]
    for first, last, far, pair, across in ((0, split, far0, pair0, across0), (split, half, far1, pair1, across1)):
        same = mine[:, first:last].astype(F32) + far[...].astype(F32)
        other = pair[...].astype(F32) + across[...].astype(F32)
        for side, branch in ((y_ref[0], same), (1 - y_ref[0], other)):
            where = pl.ds(pl.multiple_of(side * half + first, HEAD), last - first)
            out[:, where] = (hidden[:, where].astype(F32) + gate[:, where] * branch).astype(BF16)


def finish(y_lo, hidden, gate, pieces, blocks=4):
    rows, width = hidden.shape
    step = rows // blocks
    row_spec = pl.BlockSpec((step, width), lambda i, *_: (i, 0))
    return pl.pallas_call(
        finish_kernel,
        grid_spec=pltpu.PrefetchScalarGridSpec(
            num_scalar_prefetch=1,
            grid=(blocks,),
            in_specs=[row_spec, pl.BlockSpec((1, width), lambda i, *_: (0, 0))]
            + [pl.BlockSpec((step, p.shape[1]), lambda i, *_: (i, 0)) for p in pieces],
            out_specs=row_spec,
        ),
        out_shape=jax.ShapeDtypeStruct(hidden.shape, BF16),
        compiler_params=params(),
        name="finish",
    )(y_lo, hidden, gate[None], *pieces)


def shards(hidden_in, queries, keys, values, query_gain, key_gain, reach_time, reach_rows, reach_cols, out_weight, gate):
    frames, rows, nw, inner = queries.shape
    width = hidden_in.shape[3]
    weight = lax.all_gather(out_weight, "z", axis=0, tiled=False)
    tokens = [a.reshape(frames * rows, nw, inner) for a in (queries, keys, values)]
    qn, *own = prepare(*tokens, query_gain, key_gain)
    masks = mask_tables(
        lax.axis_index(TM) * frames,
        lax.axis_index(SP) * rows,
        frames * axis_size(TM),
        rows * axis_size(SP),
        nw,
    )
    combo = reach_time * 6 + reach_rows * 3 + reach_cols
    f0, f1, r0, r1 = own
    hb, ha = passed_along(f1, TM, 1), passed_along(f0, TM, -1)
    hb, ha, r0, r1, weight = lax.optimization_barrier((hb, ha, r0, r1, weight))
    weight = lax.all_gather(weight, ("x", "core"), axis=0, tiled=False)
    weight = weight.reshape((lax.axis_size("x"), lax.axis_size("core")) + weight.shape[1:])
    cb = passed_along(jnp.stack([hb[1], ha[1]]), SP, 1)
    ca = passed_along(jnp.stack([hb[0], ha[0]]), SP, -1)
    rb, ra = passed_along(r1, SP, 1), passed_along(r0, SP, -1)
    y_hi, y_lo = (lax.axis_index(a).astype(jnp.int32)[None] for a in ("y_hi", "y_lo"))
    same, other = attend(combo, y_hi, qn, (f0, f1), (hb, ha, rb, ra, cb, ca), masks)
    pair = [along_y(same, lambda y: y ^ 1), along_y(other, lambda y: 3 - y), along_y(other, lambda y: y ^ 2)]
    (mine,) = project([same], weight, 0, 4)
    pair[0], mine = lax.optimization_barrier((pair[0], mine))
    parts = []
    for first, count in ((0, 3), (3, 1)):
        to_pair, to_across, to_far = project(pair, weight, first, count)
        parts.append(
            [along_y(to_far, lambda y: y ^ 2), along_y(to_pair, lambda y: y ^ 1), along_y(to_across, lambda y: 3 - y)]
        )
        pair[0], to_far = lax.optimization_barrier((pair[0], to_far))
    pieces = [mine] + parts[0] + parts[1]
    out = finish(y_lo, hidden_in.reshape(-1, width), gate, pieces)
    return out.reshape(hidden_in.shape)


def solution(mesh):
    inner_mesh = Mesh(mesh.devices.reshape(2, 4, 2, 8, 2), TM + SP)
    tokens = P(TM, SP, None, None)
    in_specs = (tokens,) * 4 + (P(),) * 5 + (P(SP, TM), P())
    return jax.shard_map(shards, mesh=inner_mesh, in_specs=in_specs, out_specs=tokens, check_vma=False)
```

```python
import functools

import jax
import jax.numpy as jnp
from jax import lax
from jax.experimental import pallas as pl
from jax.experimental.pallas import tpu as pltpu
from jax.sharding import Mesh, PartitionSpec as P

TW = 8
HEAD = 128
TM = ("y_lo", "x")
SP = ("y_hi", "z", "core")
COMBOS = 12
F32, BF16 = jnp.float32, jnp.bfloat16


def axis_size(axes):
    n = 1
    for a in axes:
        n *= lax.axis_size(a)
    return n


def passed_along(block, axes, distance):
    n = axis_size(axes)
    route = [(i - distance, i) for i in range(n) if 0 <= i - distance < n]
    return lax.ppermute(block, axes, route)


def along_y(block, target):
    at = lambda y: (y % 2) * 2 + y // 2
    return lax.ppermute(block, ("y_lo", "y_hi"), [(at(y), at(target(y))) for y in range(4)])


def in_hbm(array):
    return pltpu.with_memory_space_constraint(array, pltpu.HBM)


def params(megabytes=24):
    return pltpu.CompilerParams(vmem_limit_bytes=megabytes << 20)


def prepare_kernel(q_ref, k_ref, v_ref, qg_ref, kg_ref, qn_ref, *outs):
    i = pl.program_id(0)
    f, r = i // 2, i % 2
    inner = q_ref.shape[-1]

    def normed(ref, gain):
        a = ref[0].astype(F32)
        ms = jnp.sum(a * a, axis=-1, keepdims=True) * (1.0 / inner)
        return (a * lax.rsqrt(ms + 1e-06) * gain[...]).astype(BF16)

    qn_ref[0] = normed(q_ref, qg_ref)
    kn = normed(k_ref, kg_ref)
    v = v_ref[0]
    f0, f1, r0, r1 = outs
    for chosen, ref in ((f == 0, f0), (f == 1, f1), (r == 0, r0), (r == 1, r1)):

        @pl.when(chosen)
        def _(ref=ref):
            ref[0, 0] = kn
            ref[0, 1] = v


def prepare(queries, keys, values, query_gain, key_gain):
    groups, nw, inner = queries.shape
    token_spec = pl.BlockSpec((1, nw, inner), lambda i: (i, 0, 0))
    gain_spec = pl.BlockSpec((1, inner), lambda i: (0, 0))
    out_shape = [pltpu.HBM(queries.shape, BF16)]
    out_specs = [token_spec]
    out_shape += [pltpu.HBM((2, 2, nw, inner), BF16)] * 4
    out_specs += [
        pl.BlockSpec((1, 2, nw, inner), lambda i: (jnp.minimum(i, 1), 0, 0, 0)),
            pl.BlockSpec((1, 2, nw, inner), lambda i: (jnp.maximum(i - 2, 0), 0, 0, 0)),
            pl.BlockSpec((1, 2, nw, inner), lambda i: (i // 2, 0, 0, 0)),
            pl.BlockSpec((1, 2, nw, inner), lambda i: (i // 2, 0, 0, 0)),
        ]
    return pl.pallas_call(
        prepare_kernel,
        grid=(groups,),
        in_specs=[token_spec] * 3 + [gain_spec] * 2,
        out_specs=out_specs,
        out_shape=out_shape,
        compiler_params=params(),
        cost_estimate=pl.CostEstimate(flops=0, bytes_accessed=12 << 20, transcendentals=0),
        name="prepare",
    )(*[in_hbm(a) for a in (queries, keys, values, query_gain[None], key_gain[None])])


def mask_tables(first_frame, first_row, frame_count, row_count, nw):
    i32 = jnp.int32
    shape = (COMBOS, 2, 2 * nw, 3 * 4 * nw)
    t = lax.broadcasted_iota(i32, shape, 0)
    f = lax.broadcasted_iota(i32, shape, 1)
    q = lax.broadcasted_iota(i32, shape, 2)
    k = lax.broadcasted_iota(i32, shape, 3)
    kf, kr, kc = k // (4 * nw), k // nw % 4, k % nw
    frame, row = first_frame - 1 + f + kf, first_row - 1 + kr
    allowed = jnp.abs(kf - 1) <= t // 6
    allowed &= jnp.abs(q // nw + 1 - kr) <= t // 3 % 2
    allowed &= jnp.abs(q % nw // TW - kc // TW) <= t % 3
    allowed &= (frame >= 0) & (frame < frame_count) & (row >= 0) & (row < row_count)
    return jnp.where(allowed, 0.0, -jnp.inf).astype(F32)


def attend_kernel(heads, scale, combo_ref, half_ref, q_ref, f0, f1, hb, ha, rb, ra, cb, ca, mask_ref, same_ref, other_ref):
    step = pl.program_id(0)
    frames = ((cb.at[0], hb, ca.at[0]), (rb.at[0], f0, ra.at[0]), (rb.at[1], f1, ra.at[1]), (cb.at[1], ha, ca.at[1]))

    def region(kv, lanes):
        parts = []
        for below, own, above in frames:
            parts += [below[kv, :, lanes], own[0, kv, :, lanes], own[1, kv, :, lanes], above[kv, :, lanes]]
        return jnp.concatenate(parts, axis=0)

    scores = {}
    for h in range(heads):
        lanes = slice(h * HEAD, (h + 1) * HEAD)
        keys = region(0, lanes)
        group = keys.shape[0] // 4
        combo = combo_ref[step * heads + h]
        for f in range(2):
            q = q_ref[2 * f : 2 * f + 2, :, lanes].reshape(-1, HEAD)
            k = keys[f * group : (f + 3) * group]
            s = lax.dot_general(q, k, (((1,), (1,)), ((), ())), preferred_element_type=F32)
            scores[h, f] = s + mask_ref[combo, f]
    weights = {}
    for at, s in scores.items():
        peak = jnp.max(s, axis=1, keepdims=True)
        w = jnp.exp((s - peak) * scale)
        weights[at] = w.astype(BF16), jnp.sum(w, axis=1, keepdims=True)
    mixed = {}
    for h in range(heads):
        lanes = slice(h * HEAD, (h + 1) * HEAD)
        values = region(1, lanes)
        group = values.shape[0] // 4
        for f in range(2):
            w, total = weights[h, f]
            o = jnp.dot(w, values[f * group : (f + 3) * group], preferred_element_type=F32)
            mixed[h, f] = (o / total).astype(BF16)
    in_half = step // (pl.num_programs(0) // 2) == half_ref[0]
    for chosen, ref in ((in_half, same_ref), (jnp.logical_not(in_half), other_ref)):

        @pl.when(chosen)
        def _(ref=ref):
            for (h, f), o in mixed.items():
                ref[f * o.shape[0] : (f + 1) * o.shape[0], h * HEAD : (h + 1) * HEAD] = o


def attend(combo, half, qn, own, halos, masks, heads=10):
    groups, nw, inner = qn.shape
    lanes = heads * HEAD
    steps = inner // lanes
    inside = steps // 2
    kv_spec = pl.BlockSpec((2, 2, nw, lanes), lambda i, *_: (0, 0, 0, i))
    same = lambda i, _, half_ref: (0, jnp.clip(i - inside * half_ref[0], 0, inside - 1))
    other = lambda i, _, half_ref: (0, jnp.clip(i - inside * (1 - half_ref[0]), 0, inside - 1))
    return pl.pallas_call(
        functools.partial(attend_kernel, heads, HEAD**-0.5),
        grid_spec=pltpu.PrefetchScalarGridSpec(
            num_scalar_prefetch=2,
            grid=(steps,),
            in_specs=[pl.BlockSpec((groups, nw, lanes), lambda i, *_: (0, 0, i))]
            + [kv_spec] * 8
            + [pl.BlockSpec(masks.shape, lambda i, *_: (0, 0, 0, 0))],
            out_specs=[pl.BlockSpec((groups * nw, lanes), same), pl.BlockSpec((groups * nw, lanes), other)],
        ),
        out_shape=[pltpu.HBM((groups * nw, inner // 2), BF16)] * 2,
        compiler_params=params(),
        cost_estimate=pl.CostEstimate(flops=4 * 128 * 384 * inner, bytes_accessed=32 << 20, transcendentals=0),
        name="attend",
    )(combo, half, qn, *own, *halos, masks)


def project_kernel(blocks, *refs):
    ins, w_ref, outs, a_buf = refs[:blocks], refs[blocks], refs[blocks + 1 : -1], refs[-1]

    @pl.when(pl.program_id(0) == 0)
    def _():
        a_buf[...] = jnp.concatenate([i[...] for i in ins], axis=0)

    _, cores, zs, _, _ = w_ref.shape
    w = jnp.concatenate([w_ref[0, c, z] for z in range(zs) for c in range(cores)], axis=0)
    term = jnp.dot(a_buf[...], w, preferred_element_type=F32)
    rows = outs[0].shape[0]
    for d, o in enumerate(outs):
        o[...] = term[d * rows : (d + 1) * rows, :].astype(BF16)


def project(blocks, weight, first, count):
    rows, depth = blocks[0].shape
    _, cores, zs, part, cols = weight.shape
    return pl.pallas_call(
        functools.partial(project_kernel, len(blocks)),
        grid=(count,),
        in_specs=[pl.BlockSpec((rows, depth), lambda j: (0, 0))] * len(blocks)
        + [pl.BlockSpec((1, cores, zs, part, cols), lambda j: (first + j, 0, 0, 0, 0))],
        out_specs=[pl.BlockSpec((rows, cols), lambda j: (0, j))] * len(blocks),
        out_shape=[jax.ShapeDtypeStruct((rows, count * cols), BF16)] * len(blocks),
        scratch_shapes=[pltpu.VMEM((len(blocks) * rows, depth), BF16)],
        compiler_params=params(32),
        cost_estimate=pl.CostEstimate(
            flops=2 * len(blocks) * rows * depth * count * cols,
            bytes_accessed=2 * depth * count * cols,
            transcendentals=0,
        ),
        name="project",
    )(*blocks, in_hbm(weight))


def finish_kernel(y_ref, hidden, gate, mine, far0, pair0, across0, far1, pair1, across1, out):
    half, split = mine.shape[-1], far0.shape[-1]
    for first, last, far, pair, across in ((0, split, far0, pair0, across0), (split, half, far1, pair1, across1)):
        same = mine[:, first:last].astype(F32) + far[...].astype(F32)
        other = pair[...].astype(F32) + across[...].astype(F32)
        for side, branch in ((y_ref[0], same), (1 - y_ref[0], other)):
            where = pl.ds(pl.multiple_of(side * half + first, HEAD), last - first)
            out[:, where] = (hidden[:, where].astype(F32) + gate[:, where] * branch).astype(BF16)


def finish(y_lo, hidden, gate, pieces, blocks=4):
    rows, width = hidden.shape
    step = rows // blocks
    row_spec = pl.BlockSpec((step, width), lambda i, *_: (i, 0))
    return pl.pallas_call(
        finish_kernel,
        grid_spec=pltpu.PrefetchScalarGridSpec(
            num_scalar_prefetch=1,
            grid=(blocks,),
            in_specs=[row_spec, pl.BlockSpec((1, width), lambda i, *_: (0, 0))]
            + [pl.BlockSpec((step, p.shape[1]), lambda i, *_: (i, 0)) for p in pieces],
            out_specs=row_spec,
        ),
        out_shape=jax.ShapeDtypeStruct(hidden.shape, BF16),
        compiler_params=params(),
        name="finish",
    )(y_lo, hidden, gate[None], *pieces)


def shards(hidden_in, queries, keys, values, query_gain, key_gain, reach_time, reach_rows, reach_cols, out_weight, gate):
    frames, rows, nw, inner = queries.shape
    width = hidden_in.shape[3]
    weight = lax.all_gather(out_weight, "z", axis=0, tiled=False)
    tokens = [a.reshape(frames * rows, nw, inner) for a in (queries, keys, values)]
    qn, *own = prepare(*tokens, query_gain, key_gain)
    masks = mask_tables(
        lax.axis_index(TM) * frames,
        lax.axis_index(SP) * rows,
        frames * axis_size(TM),
        rows * axis_size(SP),
        nw,
    )
    combo = reach_time * 6 + reach_rows * 3 + reach_cols
    f0, f1, r0, r1 = own
    hb, ha = passed_along(f1, TM, 1), passed_along(f0, TM, -1)
    hb, ha, r0, r1, weight = lax.optimization_barrier((hb, ha, r0, r1, weight))
    weight = lax.all_gather(weight, ("x", "core"), axis=0, tiled=False)
    weight = weight.reshape((lax.axis_size("x"), lax.axis_size("core")) + weight.shape[1:])
    cb = passed_along(jnp.stack([hb[1], ha[1]]), SP, 1)
    ca = passed_along(jnp.stack([hb[0], ha[0]]), SP, -1)
    rb, ra = passed_along(r1, SP, 1), passed_along(r0, SP, -1)
    y_hi, y_lo = (lax.axis_index(a).astype(jnp.int32)[None] for a in ("y_hi", "y_lo"))
    same, other = attend(combo, y_hi, qn, (f0, f1), (hb, ha, rb, ra, cb, ca), masks)
    pair = [along_y(same, lambda y: y ^ 1), along_y(other, lambda y: 3 - y), along_y(other, lambda y: y ^ 2)]
    to_pair, to_across, to_far = project(pair, weight, 0, 3)
    large = [along_y(to_far, lambda y: y ^ 2), along_y(to_pair, lambda y: y ^ 1), along_y(to_across, lambda y: 3 - y)]
    pair[0], to_far = lax.optimization_barrier((pair[0], to_far))
    to_pair, to_across, to_far = project(pair, weight, 3, 1)
    same, to_far = lax.optimization_barrier((same, to_far))
    (mine,) = project([same], weight, 0, 4)
    to_across, large[1], mine = lax.optimization_barrier((to_across, large[1], mine))
    parts = [
        large,
        [along_y(to_far, lambda y: y ^ 2), along_y(to_pair, lambda y: y ^ 1), along_y(to_across, lambda y: 3 - y)],
    ]
    pieces = [mine] + parts[0] + parts[1]
    out = finish(y_lo, hidden_in.reshape(-1, width), gate, pieces)
    return out.reshape(hidden_in.shape)


def solution(mesh):
    inner_mesh = Mesh(mesh.devices.reshape(2, 4, 2, 8, 2), TM + SP)
    tokens = P(TM, SP, None, None)
    in_specs = (tokens,) * 4 + (P(),) * 5 + (P(SP, TM), P())
    return jax.shard_map(shards, mesh=inner_mesh, in_specs=in_specs, out_specs=tokens, check_vma=False)
```

```python
import functools

import jax
import jax.numpy as jnp
from jax import lax
from jax.experimental import pallas as pl
from jax.experimental.pallas import tpu as pltpu
from jax.sharding import Mesh, PartitionSpec as P

TW = 8
HEAD = 128
TM = ("y_lo", "x")
SP = ("y_hi", "z", "core")
COMBOS = 12
F32, BF16 = jnp.float32, jnp.bfloat16


def axis_size(axes):
    n = 1
    for a in axes:
        n *= lax.axis_size(a)
    return n


def passed_along(block, axes, distance):
    n = axis_size(axes)
    route = [(i - distance, i) for i in range(n) if 0 <= i - distance < n]
    return lax.ppermute(block, axes, route)


def along_y(block, target):
    at = lambda y: (y % 2) * 2 + y // 2
    return lax.ppermute(block, ("y_lo", "y_hi"), [(at(y), at(target(y))) for y in range(4)])


def in_hbm(array):
    return pltpu.with_memory_space_constraint(array, pltpu.HBM)


def params(megabytes=24):
    return pltpu.CompilerParams(vmem_limit_bytes=megabytes << 20)


def prepare_kernel(q_ref, k_ref, v_ref, qg_ref, kg_ref, qn_ref, *outs):
    i = pl.program_id(0)
    f, r = i // 2, i % 2
    inner = q_ref.shape[-1]

    def normed(ref, gain):
        a = ref[0].astype(F32)
        ms = jnp.sum(a * a, axis=-1, keepdims=True) * (1.0 / inner)
        return (a * lax.rsqrt(ms + 1e-06) * gain[...]).astype(BF16)

    qn_ref[0] = normed(q_ref, qg_ref)
    kn = normed(k_ref, kg_ref)
    v = v_ref[0]
    f0, f1, r0, r1 = outs
    for chosen, ref in ((f == 0, f0), (f == 1, f1), (r == 0, r0), (r == 1, r1)):

        @pl.when(chosen)
        def _(ref=ref):
            ref[0, 0] = kn
            ref[0, 1] = v


def prepare(queries, keys, values, query_gain, key_gain):
    groups, nw, inner = queries.shape
    token_spec = pl.BlockSpec((1, nw, inner), lambda i: (i, 0, 0))
    gain_spec = pl.BlockSpec((1, inner), lambda i: (0, 0))
    out_shape = [pltpu.HBM(queries.shape, BF16)]
    out_specs = [token_spec]
    out_shape += [pltpu.HBM((2, 2, nw, inner), BF16)] * 4
    out_specs += [
        pl.BlockSpec((1, 2, nw, inner), lambda i: (jnp.minimum(i, 1), 0, 0, 0)),
            pl.BlockSpec((1, 2, nw, inner), lambda i: (jnp.maximum(i - 2, 0), 0, 0, 0)),
            pl.BlockSpec((1, 2, nw, inner), lambda i: (i // 2, 0, 0, 0)),
            pl.BlockSpec((1, 2, nw, inner), lambda i: (i // 2, 0, 0, 0)),
        ]
    return pl.pallas_call(
        prepare_kernel,
        grid=(groups,),
        in_specs=[token_spec] * 3 + [gain_spec] * 2,
        out_specs=out_specs,
        out_shape=out_shape,
        compiler_params=params(),
        cost_estimate=pl.CostEstimate(flops=0, bytes_accessed=12 << 20, transcendentals=0),
        name="prepare",
    )(*[in_hbm(a) for a in (queries, keys, values, query_gain[None], key_gain[None])])


def mask_tables(first_frame, first_row, frame_count, row_count, nw):
    i32 = jnp.int32
    shape = (COMBOS, 2, 2 * nw, 3 * 4 * nw)
    t = lax.broadcasted_iota(i32, shape, 0)
    f = lax.broadcasted_iota(i32, shape, 1)
    q = lax.broadcasted_iota(i32, shape, 2)
    k = lax.broadcasted_iota(i32, shape, 3)
    kf, kr, kc = k // (4 * nw), k // nw % 4, k % nw
    frame, row = first_frame - 1 + f + kf, first_row - 1 + kr
    allowed = jnp.abs(kf - 1) <= t // 6
    allowed &= jnp.abs(q // nw + 1 - kr) <= t // 3 % 2
    allowed &= jnp.abs(q % nw // TW - kc // TW) <= t % 3
    allowed &= (frame >= 0) & (frame < frame_count) & (row >= 0) & (row < row_count)
    return jnp.where(allowed, 0.0, -jnp.inf).astype(F32)


def attend_kernel(heads, scale, combo_ref, half_ref, q_ref, f0, f1, hb, ha, rb, ra, cb, ca, mask_ref, same_ref, other_ref):
    step = pl.program_id(0)
    frames = ((cb.at[0], hb, ca.at[0]), (rb.at[0], f0, ra.at[0]), (rb.at[1], f1, ra.at[1]), (cb.at[1], ha, ca.at[1]))

    def region(kv, lanes):
        parts = []
        for below, own, above in frames:
            parts += [below[kv, :, lanes], own[0, kv, :, lanes], own[1, kv, :, lanes], above[kv, :, lanes]]
        return jnp.concatenate(parts, axis=0)

    scores = {}
    for h in range(heads):
        lanes = slice(h * HEAD, (h + 1) * HEAD)
        keys = region(0, lanes)
        group = keys.shape[0] // 4
        combo = combo_ref[step * heads + h]
        for f in range(2):
            q = q_ref[2 * f : 2 * f + 2, :, lanes].reshape(-1, HEAD)
            k = keys[f * group : (f + 3) * group]
            s = lax.dot_general(q, k, (((1,), (1,)), ((), ())), preferred_element_type=F32)
            scores[h, f] = s + mask_ref[combo, f]
    weights = {}
    for at, s in scores.items():
        peak = jnp.max(s, axis=1, keepdims=True)
        w = jnp.exp((s - peak) * scale)
        weights[at] = w.astype(BF16), jnp.sum(w, axis=1, keepdims=True)
    mixed = {}
    for h in range(heads):
        lanes = slice(h * HEAD, (h + 1) * HEAD)
        values = region(1, lanes)
        group = values.shape[0] // 4
        for f in range(2):
            w, total = weights[h, f]
            o = jnp.dot(w, values[f * group : (f + 3) * group], preferred_element_type=F32)
            mixed[h, f] = (o / total).astype(BF16)
    in_half = step // (pl.num_programs(0) // 2) == half_ref[0]
    for chosen, ref in ((in_half, same_ref), (jnp.logical_not(in_half), other_ref)):

        @pl.when(chosen)
        def _(ref=ref):
            for (h, f), o in mixed.items():
                ref[f * o.shape[0] : (f + 1) * o.shape[0], h * HEAD : (h + 1) * HEAD] = o


def attend(combo, half, qn, own, halos, masks, heads=10):
    groups, nw, inner = qn.shape
    lanes = heads * HEAD
    steps = inner // lanes
    inside = steps // 2
    kv_spec = pl.BlockSpec((2, 2, nw, lanes), lambda i, *_: (0, 0, 0, i))
    same = lambda i, _, half_ref: (0, jnp.clip(i - inside * half_ref[0], 0, inside - 1))
    other = lambda i, _, half_ref: (0, jnp.clip(i - inside * (1 - half_ref[0]), 0, inside - 1))
    return pl.pallas_call(
        functools.partial(attend_kernel, heads, HEAD**-0.5),
        grid_spec=pltpu.PrefetchScalarGridSpec(
            num_scalar_prefetch=2,
            grid=(steps,),
            in_specs=[pl.BlockSpec((groups, nw, lanes), lambda i, *_: (0, 0, i))]
            + [kv_spec] * 8
            + [pl.BlockSpec(masks.shape, lambda i, *_: (0, 0, 0, 0))],
            out_specs=[pl.BlockSpec((groups * nw, lanes), same), pl.BlockSpec((groups * nw, lanes), other)],
        ),
        out_shape=[pltpu.HBM((groups * nw, inner // 2), BF16)] * 2,
        compiler_params=params(),
        cost_estimate=pl.CostEstimate(flops=4 * 128 * 384 * inner, bytes_accessed=32 << 20, transcendentals=0),
        name="attend",
    )(combo, half, qn, *own, *halos, masks)


def project_kernel(blocks, *refs):
    ins, w_ref, outs, a_buf = refs[:blocks], refs[blocks], refs[blocks + 1 : -1], refs[-1]

    @pl.when(pl.program_id(0) == 0)
    def _():
        a_buf[...] = jnp.concatenate([i[...] for i in ins], axis=0)

    _, cores, zs, _, _ = w_ref.shape
    w = jnp.concatenate([w_ref[0, c, z] for z in range(zs) for c in range(cores)], axis=0)
    term = jnp.dot(a_buf[...], w, preferred_element_type=F32)
    rows = outs[0].shape[0]
    for d, o in enumerate(outs):
        o[...] = term[d * rows : (d + 1) * rows, :].astype(BF16)


def project(blocks, weight, first, count):
    rows, depth = blocks[0].shape
    _, cores, zs, part, cols = weight.shape
    return pl.pallas_call(
        functools.partial(project_kernel, len(blocks)),
        grid=(count,),
        in_specs=[pl.BlockSpec((rows, depth), lambda j: (0, 0))] * len(blocks)
        + [pl.BlockSpec((1, cores, zs, part, cols), lambda j: (first + j, 0, 0, 0, 0))],
        out_specs=[pl.BlockSpec((rows, cols), lambda j: (0, j))] * len(blocks),
        out_shape=[jax.ShapeDtypeStruct((rows, count * cols), BF16)] * len(blocks),
        scratch_shapes=[pltpu.VMEM((len(blocks) * rows, depth), BF16)],
        compiler_params=params(32),
        cost_estimate=pl.CostEstimate(
            flops=2 * len(blocks) * rows * depth * count * cols,
            bytes_accessed=2 * depth * count * cols,
            transcendentals=0,
        ),
        name="project",
    )(*blocks, in_hbm(weight))


def finish_kernel(y_ref, hidden, gate, mine, far0, pair0, across0, far1, pair1, across1, out):
    half, split = mine.shape[-1], far0.shape[-1]
    for first, last, far, pair, across in ((0, split, far0, pair0, across0), (split, half, far1, pair1, across1)):
        same = mine[:, first:last].astype(F32) + far[...].astype(F32)
        other = pair[...].astype(F32) + across[...].astype(F32)
        for side, branch in ((y_ref[0], same), (1 - y_ref[0], other)):
            where = pl.ds(pl.multiple_of(side * half + first, HEAD), last - first)
            out[:, where] = (hidden[:, where].astype(F32) + gate[:, where] * branch).astype(BF16)


def finish(y_lo, hidden, gate, pieces, blocks=4):
    rows, width = hidden.shape
    step = rows // blocks
    row_spec = pl.BlockSpec((step, width), lambda i, *_: (i, 0))
    return pl.pallas_call(
        finish_kernel,
        grid_spec=pltpu.PrefetchScalarGridSpec(
            num_scalar_prefetch=1,
            grid=(blocks,),
            in_specs=[row_spec, pl.BlockSpec((1, width), lambda i, *_: (0, 0))]
            + [pl.BlockSpec((step, p.shape[1]), lambda i, *_: (i, 0)) for p in pieces],
            out_specs=row_spec,
        ),
        out_shape=jax.ShapeDtypeStruct(hidden.shape, BF16),
        compiler_params=params(),
        name="finish",
    )(y_lo, hidden, gate[None], *pieces)


def shards(hidden_in, queries, keys, values, query_gain, key_gain, reach_time, reach_rows, reach_cols, out_weight, gate):
    frames, rows, nw, inner = queries.shape
    width = hidden_in.shape[3]
    weight = lax.all_gather(out_weight, "z", axis=0, tiled=False)
    tokens = [a.reshape(frames * rows, nw, inner) for a in (queries, keys, values)]
    qn, *own = prepare(*tokens, query_gain, key_gain)
    masks = mask_tables(
        lax.axis_index(TM) * frames,
        lax.axis_index(SP) * rows,
        frames * axis_size(TM),
        rows * axis_size(SP),
        nw,
    )
    combo = reach_time * 6 + reach_rows * 3 + reach_cols
    f0, f1, r0, r1 = own
    hb, ha = passed_along(f1, TM, 1), passed_along(f0, TM, -1)
    hb, ha, r0, r1, weight = lax.optimization_barrier((hb, ha, r0, r1, weight))
    weight = lax.all_gather(weight, ("x", "core"), axis=0, tiled=False)
    weight = weight.reshape((lax.axis_size("x"), lax.axis_size("core")) + weight.shape[1:])
    cb = passed_along(jnp.stack([hb[1], ha[1]]), SP, 1)
    ca = passed_along(jnp.stack([hb[0], ha[0]]), SP, -1)
    rb, ra = passed_along(r1, SP, 1), passed_along(r0, SP, -1)
    y_hi, y_lo = (lax.axis_index(a).astype(jnp.int32)[None] for a in ("y_hi", "y_lo"))
    same, other = attend(combo, y_hi, qn, (f0, f1), (hb, ha, rb, ra, cb, ca), masks)
    pair = [along_y(same, lambda y: y ^ 1), along_y(other, lambda y: 3 - y), along_y(other, lambda y: y ^ 2)]
    to_pair, to_across, to_far = project(pair, weight, 0, 2)
    large = [along_y(to_far, lambda y: y ^ 2), along_y(to_pair, lambda y: y ^ 1), along_y(to_across, lambda y: 3 - y)]
    pair[0], to_far = lax.optimization_barrier((pair[0], to_far))
    to_pair, to_across, to_far = project(pair, weight, 2, 2)
    same, to_far = lax.optimization_barrier((same, to_far))
    (mine,) = project([same], weight, 0, 4)
    to_across, large[1], large[2], mine = lax.optimization_barrier((to_across, large[1], large[2], mine))
    parts = [
        large,
        [along_y(to_far, lambda y: y ^ 2), along_y(to_pair, lambda y: y ^ 1), along_y(to_across, lambda y: 3 - y)],
    ]
    pieces = [mine] + parts[0] + parts[1]
    out = finish(y_lo, hidden_in.reshape(-1, width), gate, pieces)
    return out.reshape(hidden_in.shape)


def solution(mesh):
    inner_mesh = Mesh(mesh.devices.reshape(2, 4, 2, 8, 2), TM + SP)
    tokens = P(TM, SP, None, None)
    in_specs = (tokens,) * 4 + (P(),) * 5 + (P(SP, TM), P())
    return jax.shard_map(shards, mesh=inner_mesh, in_specs=in_specs, out_specs=tokens, check_vma=False)
```

```python
import functools

import jax
import jax.numpy as jnp
from jax import lax
from jax.experimental import pallas as pl
from jax.experimental.pallas import tpu as pltpu
from jax.sharding import Mesh, PartitionSpec as P

TW = 8
HEAD = 128
TM = ("y_lo", "x")
SP = ("y_hi", "z", "core")
COMBOS = 12
F32, BF16 = jnp.float32, jnp.bfloat16


def axis_size(axes):
    n = 1
    for a in axes:
        n *= lax.axis_size(a)
    return n


def passed_along(block, axes, distance):
    n = axis_size(axes)
    route = [(i - distance, i) for i in range(n) if 0 <= i - distance < n]
    return lax.ppermute(block, axes, route)


def along_y(block, target):
    at = lambda y: (y % 2) * 2 + y // 2
    return lax.ppermute(block, ("y_lo", "y_hi"), [(at(y), at(target(y))) for y in range(4)])


def in_hbm(array):
    return pltpu.with_memory_space_constraint(array, pltpu.HBM)


def params(megabytes=24):
    return pltpu.CompilerParams(vmem_limit_bytes=megabytes << 20)


def prepare_kernel(q_ref, k_ref, v_ref, qg_ref, kg_ref, qn_ref, *outs):
    i = pl.program_id(0)
    f, r = i // 2, i % 2
    inner = q_ref.shape[-1]

    def normed(ref, gain):
        a = ref[0].astype(F32)
        ms = jnp.sum(a * a, axis=-1, keepdims=True) * (1.0 / inner)
        return (a * lax.rsqrt(ms + 1e-06) * gain[...]).astype(BF16)

    qn_ref[0] = normed(q_ref, qg_ref)
    kn = normed(k_ref, kg_ref)
    v = v_ref[0]
    f0, f1, r0, r1 = outs
    for chosen, ref in ((f == 0, f0), (f == 1, f1), (r == 0, r0), (r == 1, r1)):

        @pl.when(chosen)
        def _(ref=ref):
            ref[0, 0] = kn
            ref[0, 1] = v


def prepare(queries, keys, values, query_gain, key_gain):
    groups, nw, inner = queries.shape
    token_spec = pl.BlockSpec((1, nw, inner), lambda i: (i, 0, 0))
    gain_spec = pl.BlockSpec((1, inner), lambda i: (0, 0))
    out_shape = [pltpu.HBM(queries.shape, BF16)]
    out_specs = [token_spec]
    out_shape += [pltpu.HBM((2, 2, nw, inner), BF16)] * 4
    out_specs += [
        pl.BlockSpec((1, 2, nw, inner), lambda i: (jnp.minimum(i, 1), 0, 0, 0)),
            pl.BlockSpec((1, 2, nw, inner), lambda i: (jnp.maximum(i - 2, 0), 0, 0, 0)),
            pl.BlockSpec((1, 2, nw, inner), lambda i: (i // 2, 0, 0, 0)),
            pl.BlockSpec((1, 2, nw, inner), lambda i: (i // 2, 0, 0, 0)),
        ]
    return pl.pallas_call(
        prepare_kernel,
        grid=(groups,),
        in_specs=[token_spec] * 3 + [gain_spec] * 2,
        out_specs=out_specs,
        out_shape=out_shape,
        compiler_params=params(),
        cost_estimate=pl.CostEstimate(flops=0, bytes_accessed=12 << 20, transcendentals=0),
        name="prepare",
    )(*[in_hbm(a) for a in (queries, keys, values, query_gain[None], key_gain[None])])


def mask_tables(first_frame, first_row, frame_count, row_count, nw):
    i32 = jnp.int32
    shape = (COMBOS, 2, 2 * nw, 3 * 4 * nw)
    t = lax.broadcasted_iota(i32, shape, 0)
    f = lax.broadcasted_iota(i32, shape, 1)
    q = lax.broadcasted_iota(i32, shape, 2)
    k = lax.broadcasted_iota(i32, shape, 3)
    kf, kr, kc = k // (4 * nw), k // nw % 4, k % nw
    frame, row = first_frame - 1 + f + kf, first_row - 1 + kr
    allowed = jnp.abs(kf - 1) <= t // 6
    allowed &= jnp.abs(q // nw + 1 - kr) <= t // 3 % 2
    allowed &= jnp.abs(q % nw // TW - kc // TW) <= t % 3
    allowed &= (frame >= 0) & (frame < frame_count) & (row >= 0) & (row < row_count)
    return jnp.where(allowed, 0.0, -jnp.inf).astype(F32)


def attend_kernel(heads, scale, combo_ref, half_ref, q_ref, f0, f1, hb, ha, rb, ra, cb, ca, mask_ref, same_ref, other_ref):
    step = pl.program_id(0)
    frames = ((cb.at[0], hb, ca.at[0]), (rb.at[0], f0, ra.at[0]), (rb.at[1], f1, ra.at[1]), (cb.at[1], ha, ca.at[1]))

    def region(kv, lanes):
        parts = []
        for below, own, above in frames:
            parts += [below[kv, :, lanes], own[0, kv, :, lanes], own[1, kv, :, lanes], above[kv, :, lanes]]
        return jnp.concatenate(parts, axis=0)

    scores = {}
    for h in range(heads):
        lanes = slice(h * HEAD, (h + 1) * HEAD)
        keys = region(0, lanes)
        group = keys.shape[0] // 4
        combo = combo_ref[step * heads + h]
        for f in range(2):
            q = q_ref[2 * f : 2 * f + 2, :, lanes].reshape(-1, HEAD)
            k = keys[f * group : (f + 3) * group]
            s = lax.dot_general(q, k, (((1,), (1,)), ((), ())), preferred_element_type=F32)
            scores[h, f] = s + mask_ref[combo, f]
    weights = {}
    for at, s in scores.items():
        peak = jnp.max(s, axis=1, keepdims=True)
        w = jnp.exp((s - peak) * scale)
        weights[at] = w.astype(BF16), jnp.sum(w, axis=1, keepdims=True)
    mixed = {}
    for h in range(heads):
        lanes = slice(h * HEAD, (h + 1) * HEAD)
        values = region(1, lanes)
        group = values.shape[0] // 4
        for f in range(2):
            w, total = weights[h, f]
            o = jnp.dot(w, values[f * group : (f + 3) * group], preferred_element_type=F32)
            mixed[h, f] = (o / total).astype(BF16)
    in_half = step // (pl.num_programs(0) // 2) == half_ref[0]
    for chosen, ref in ((in_half, same_ref), (jnp.logical_not(in_half), other_ref)):

        @pl.when(chosen)
        def _(ref=ref):
            for (h, f), o in mixed.items():
                ref[f * o.shape[0] : (f + 1) * o.shape[0], h * HEAD : (h + 1) * HEAD] = o


def attend(combo, half, qn, own, halos, masks, heads=10):
    groups, nw, inner = qn.shape
    lanes = heads * HEAD
    steps = inner // lanes
    inside = steps // 2
    kv_spec = pl.BlockSpec((2, 2, nw, lanes), lambda i, *_: (0, 0, 0, i))
    same = lambda i, _, half_ref: (0, jnp.clip(i - inside * half_ref[0], 0, inside - 1))
    other = lambda i, _, half_ref: (0, jnp.clip(i - inside * (1 - half_ref[0]), 0, inside - 1))
    return pl.pallas_call(
        functools.partial(attend_kernel, heads, HEAD**-0.5),
        grid_spec=pltpu.PrefetchScalarGridSpec(
            num_scalar_prefetch=2,
            grid=(steps,),
            in_specs=[pl.BlockSpec((groups, nw, lanes), lambda i, *_: (0, 0, i))]
            + [kv_spec] * 8
            + [pl.BlockSpec(masks.shape, lambda i, *_: (0, 0, 0, 0))],
            out_specs=[pl.BlockSpec((groups * nw, lanes), same), pl.BlockSpec((groups * nw, lanes), other)],
        ),
        out_shape=[pltpu.HBM((groups * nw, inner // 2), BF16)] * 2,
        compiler_params=params(),
        cost_estimate=pl.CostEstimate(flops=4 * 128 * 384 * inner, bytes_accessed=32 << 20, transcendentals=0),
        name="attend",
    )(combo, half, qn, *own, *halos, masks)


def project_kernel(blocks, *refs):
    ins, w_ref, outs, a_buf = refs[:blocks], refs[blocks], refs[blocks + 1 : -1], refs[-1]

    @pl.when(pl.program_id(0) == 0)
    def _():
        a_buf[...] = jnp.concatenate([i[...] for i in ins], axis=0)

    _, cores, zs, _, _ = w_ref.shape
    w = jnp.concatenate([w_ref[0, c, z] for z in range(zs) for c in range(cores)], axis=0)
    term = jnp.dot(a_buf[...], w, preferred_element_type=F32)
    rows = outs[0].shape[0]
    for d, o in enumerate(outs):
        o[...] = term[d * rows : (d + 1) * rows, :].astype(BF16)


def project(blocks, weight, first, count):
    rows, depth = blocks[0].shape
    _, cores, zs, part, cols = weight.shape
    return pl.pallas_call(
        functools.partial(project_kernel, len(blocks)),
        grid=(count,),
        in_specs=[pl.BlockSpec((rows, depth), lambda j: (0, 0))] * len(blocks)
        + [pl.BlockSpec((1, cores, zs, part, cols), lambda j: (first + j, 0, 0, 0, 0))],
        out_specs=[pl.BlockSpec((rows, cols), lambda j: (0, j))] * len(blocks),
        out_shape=[jax.ShapeDtypeStruct((rows, count * cols), BF16)] * len(blocks),
        scratch_shapes=[pltpu.VMEM((len(blocks) * rows, depth), BF16)],
        compiler_params=params(32),
        cost_estimate=pl.CostEstimate(
            flops=2 * len(blocks) * rows * depth * count * cols,
            bytes_accessed=2 * depth * count * cols,
            transcendentals=0,
        ),
        name="project",
    )(*blocks, in_hbm(weight))


def finish_kernel(y_ref, hidden, gate, mine, far0, pair0, across0, far1, pair1, across1, out):
    half, split = mine.shape[-1], far0.shape[-1]
    for first, last, far, pair, across in ((0, split, far0, pair0, across0), (split, half, far1, pair1, across1)):
        same = mine[:, first:last].astype(F32) + far[...].astype(F32)
        other = pair[...].astype(F32) + across[...].astype(F32)
        for side, branch in ((y_ref[0], same), (1 - y_ref[0], other)):
            where = pl.ds(pl.multiple_of(side * half + first, HEAD), last - first)
            out[:, where] = (hidden[:, where].astype(F32) + gate[:, where] * branch).astype(BF16)


def finish(y_lo, hidden, gate, pieces, blocks=4):
    rows, width = hidden.shape
    step = rows // blocks
    row_spec = pl.BlockSpec((step, width), lambda i, *_: (i, 0))
    return pl.pallas_call(
        finish_kernel,
        grid_spec=pltpu.PrefetchScalarGridSpec(
            num_scalar_prefetch=1,
            grid=(blocks,),
            in_specs=[row_spec, pl.BlockSpec((1, width), lambda i, *_: (0, 0))]
            + [pl.BlockSpec((step, p.shape[1]), lambda i, *_: (i, 0)) for p in pieces],
            out_specs=row_spec,
        ),
        out_shape=jax.ShapeDtypeStruct(hidden.shape, BF16),
        compiler_params=params(),
        name="finish",
    )(y_lo, hidden, gate[None], *pieces)


def shards(hidden_in, queries, keys, values, query_gain, key_gain, reach_time, reach_rows, reach_cols, out_weight, gate):
    frames, rows, nw, inner = queries.shape
    width = hidden_in.shape[3]
    weight = lax.all_gather(out_weight, "z", axis=0, tiled=False)
    tokens = [a.reshape(frames * rows, nw, inner) for a in (queries, keys, values)]
    qn, *own = prepare(*tokens, query_gain, key_gain)
    masks = mask_tables(
        lax.axis_index(TM) * frames,
        lax.axis_index(SP) * rows,
        frames * axis_size(TM),
        rows * axis_size(SP),
        nw,
    )
    combo = reach_time * 6 + reach_rows * 3 + reach_cols
    f0, f1, r0, r1 = own
    hb, ha = passed_along(f1, TM, 1), passed_along(f0, TM, -1)
    hb, ha, r0, r1, weight = lax.optimization_barrier((hb, ha, r0, r1, weight))
    weight = lax.all_gather(weight, ("x", "core"), axis=0, tiled=False)
    weight = weight.reshape((lax.axis_size("x"), lax.axis_size("core")) + weight.shape[1:])
    cb = passed_along(jnp.stack([hb[1], ha[1]]), SP, 1)
    ca = passed_along(jnp.stack([hb[0], ha[0]]), SP, -1)
    rb, ra = passed_along(r1, SP, 1), passed_along(r0, SP, -1)
    y_hi, y_lo = (lax.axis_index(a).astype(jnp.int32)[None] for a in ("y_hi", "y_lo"))
    same, other = attend(combo, y_hi, qn, (f0, f1), (hb, ha, rb, ra, cb, ca), masks)
    pair = [along_y(same, lambda y: y ^ 1), along_y(other, lambda y: 3 - y), along_y(other, lambda y: y ^ 2)]
    to_pair, to_across, to_far = project(pair, weight, 0, 2)
    large = [along_y(to_far, lambda y: y ^ 2), along_y(to_pair, lambda y: y ^ 1), along_y(to_across, lambda y: 3 - y)]
    pair[0], to_far = lax.optimization_barrier((pair[0], to_far))
    to_pair, to_across, to_far = project(pair, weight, 2, 2)
    same, to_far = lax.optimization_barrier((same, to_far))
    (mine,) = project([same], weight, 0, 4)
    to_across, large[1], large[2] = lax.optimization_barrier((to_across, large[1], large[2]))
    parts = [
        large,
        [along_y(to_far, lambda y: y ^ 2), along_y(to_pair, lambda y: y ^ 1), along_y(to_across, lambda y: 3 - y)],
    ]
    pieces = [mine] + parts[0] + parts[1]
    out = finish(y_lo, hidden_in.reshape(-1, width), gate, pieces)
    return out.reshape(hidden_in.shape)


def solution(mesh):
    inner_mesh = Mesh(mesh.devices.reshape(2, 4, 2, 8, 2), TM + SP)
    tokens = P(TM, SP, None, None)
    in_specs = (tokens,) * 4 + (P(),) * 5 + (P(SP, TM), P())
    return jax.shard_map(shards, mesh=inner_mesh, in_specs=in_specs, out_specs=tokens, check_vma=False)
```

```python
import functools

import jax
import jax.numpy as jnp
from jax import lax
from jax.experimental import pallas as pl
from jax.experimental.pallas import tpu as pltpu
from jax.sharding import Mesh, PartitionSpec as P

TW = 8
HEAD = 128
TM = ("y_lo", "x")
SP = ("y_hi", "z", "core")
COMBOS = 12
F32, BF16 = jnp.float32, jnp.bfloat16


def axis_size(axes):
    n = 1
    for a in axes:
        n *= lax.axis_size(a)
    return n


def passed_along(block, axes, distance):
    n = axis_size(axes)
    route = [(i - distance, i) for i in range(n) if 0 <= i - distance < n]
    return lax.ppermute(block, axes, route)


def along_y(block, target):
    at = lambda y: (y % 2) * 2 + y // 2
    return lax.ppermute(block, ("y_lo", "y_hi"), [(at(y), at(target(y))) for y in range(4)])


def in_hbm(array):
    return pltpu.with_memory_space_constraint(array, pltpu.HBM)


def params(megabytes=24):
    return pltpu.CompilerParams(vmem_limit_bytes=megabytes << 20)


def prepare_kernel(q_ref, k_ref, v_ref, qg_ref, kg_ref, qn_ref, *outs):
    i = pl.program_id(0)
    f, r = i // 2, i % 2
    inner = q_ref.shape[-1]

    def normed(ref, gain):
        a = ref[0].astype(F32)
        ms = jnp.sum(a * a, axis=-1, keepdims=True) * (1.0 / inner)
        return (a * lax.rsqrt(ms + 1e-06) * gain[...]).astype(BF16)

    qn_ref[0] = normed(q_ref, qg_ref)
    kn = normed(k_ref, kg_ref)
    v = v_ref[0]
    f0, f1, r0, r1 = outs
    for chosen, ref in ((f == 0, f0), (f == 1, f1), (r == 0, r0), (r == 1, r1)):

        @pl.when(chosen)
        def _(ref=ref):
            ref[0, 0] = kn
            ref[0, 1] = v


def prepare(queries, keys, values, query_gain, key_gain):
    groups, nw, inner = queries.shape
    token_spec = pl.BlockSpec((1, nw, inner), lambda i: (i, 0, 0))
    gain_spec = pl.BlockSpec((1, inner), lambda i: (0, 0))
    out_shape = [pltpu.HBM(queries.shape, BF16)]
    out_specs = [token_spec]
    out_shape += [pltpu.HBM((2, 2, nw, inner), BF16)] * 4
    out_specs += [
        pl.BlockSpec((1, 2, nw, inner), lambda i: (jnp.minimum(i, 1), 0, 0, 0)),
            pl.BlockSpec((1, 2, nw, inner), lambda i: (jnp.maximum(i - 2, 0), 0, 0, 0)),
            pl.BlockSpec((1, 2, nw, inner), lambda i: (i // 2, 0, 0, 0)),
            pl.BlockSpec((1, 2, nw, inner), lambda i: (i // 2, 0, 0, 0)),
        ]
    return pl.pallas_call(
        prepare_kernel,
        grid=(groups,),
        in_specs=[token_spec] * 3 + [gain_spec] * 2,
        out_specs=out_specs,
        out_shape=out_shape,
        compiler_params=params(),
        cost_estimate=pl.CostEstimate(flops=0, bytes_accessed=12 << 20, transcendentals=0),
        name="prepare",
    )(*[in_hbm(a) for a in (queries, keys, values, query_gain[None], key_gain[None])])


def mask_tables(first_frame, first_row, frame_count, row_count, nw):
    i32 = jnp.int32
    shape = (COMBOS, 2, 2 * nw, 3 * 4 * nw)
    t = lax.broadcasted_iota(i32, shape, 0)
    f = lax.broadcasted_iota(i32, shape, 1)
    q = lax.broadcasted_iota(i32, shape, 2)
    k = lax.broadcasted_iota(i32, shape, 3)
    kf, kr, kc = k // (4 * nw), k // nw % 4, k % nw
    frame, row = first_frame - 1 + f + kf, first_row - 1 + kr
    allowed = jnp.abs(kf - 1) <= t // 6
    allowed &= jnp.abs(q // nw + 1 - kr) <= t // 3 % 2
    allowed &= jnp.abs(q % nw // TW - kc // TW) <= t % 3
    allowed &= (frame >= 0) & (frame < frame_count) & (row >= 0) & (row < row_count)
    return jnp.where(allowed, 0.0, -jnp.inf).astype(F32)


def attend_kernel(heads, scale, combo_ref, half_ref, q_ref, f0, f1, hb, ha, rb, ra, cb, ca, mask_ref, same_ref, other_ref):
    step = pl.program_id(0)
    frames = ((cb.at[0], hb, ca.at[0]), (rb.at[0], f0, ra.at[0]), (rb.at[1], f1, ra.at[1]), (cb.at[1], ha, ca.at[1]))

    def region(kv, lanes):
        parts = []
        for below, own, above in frames:
            parts += [below[kv, :, lanes], own[0, kv, :, lanes], own[1, kv, :, lanes], above[kv, :, lanes]]
        return jnp.concatenate(parts, axis=0)

    scores = {}
    for h in range(heads):
        lanes = slice(h * HEAD, (h + 1) * HEAD)
        keys = region(0, lanes)
        group = keys.shape[0] // 4
        combo = combo_ref[step * heads + h]
        for f in range(2):
            q = q_ref[2 * f : 2 * f + 2, :, lanes].reshape(-1, HEAD)
            k = keys[f * group : (f + 3) * group]
            s = lax.dot_general(q, k, (((1,), (1,)), ((), ())), preferred_element_type=F32)
            scores[h, f] = s + mask_ref[combo, f]
    weights = {}
    for at, s in scores.items():
        peak = jnp.max(s, axis=1, keepdims=True)
        w = jnp.exp((s - peak) * scale)
        weights[at] = w.astype(BF16), jnp.sum(w, axis=1, keepdims=True)
    mixed = {}
    for h in range(heads):
        lanes = slice(h * HEAD, (h + 1) * HEAD)
        values = region(1, lanes)
        group = values.shape[0] // 4
        for f in range(2):
            w, total = weights[h, f]
            o = jnp.dot(w, values[f * group : (f + 3) * group], preferred_element_type=F32)
            mixed[h, f] = (o / total).astype(BF16)
    in_half = step // (pl.num_programs(0) // 2) == half_ref[0]
    for chosen, ref in ((in_half, same_ref), (jnp.logical_not(in_half), other_ref)):

        @pl.when(chosen)
        def _(ref=ref):
            for (h, f), o in mixed.items():
                ref[f * o.shape[0] : (f + 1) * o.shape[0], h * HEAD : (h + 1) * HEAD] = o


def attend(combo, half, qn, own, halos, masks, heads=10):
    groups, nw, inner = qn.shape
    lanes = heads * HEAD
    steps = inner // lanes
    inside = steps // 2
    kv_spec = pl.BlockSpec((2, 2, nw, lanes), lambda i, *_: (0, 0, 0, i))
    same = lambda i, _, half_ref: (0, jnp.clip(i - inside * half_ref[0], 0, inside - 1))
    other = lambda i, _, half_ref: (0, jnp.clip(i - inside * (1 - half_ref[0]), 0, inside - 1))
    return pl.pallas_call(
        functools.partial(attend_kernel, heads, HEAD**-0.5),
        grid_spec=pltpu.PrefetchScalarGridSpec(
            num_scalar_prefetch=2,
            grid=(steps,),
            in_specs=[pl.BlockSpec((groups, nw, lanes), lambda i, *_: (0, 0, i))]
            + [kv_spec] * 8
            + [pl.BlockSpec(masks.shape, lambda i, *_: (0, 0, 0, 0))],
            out_specs=[pl.BlockSpec((groups * nw, lanes), same), pl.BlockSpec((groups * nw, lanes), other)],
        ),
        out_shape=[pltpu.HBM((groups * nw, inner // 2), BF16)] * 2,
        compiler_params=params(),
        cost_estimate=pl.CostEstimate(flops=4 * 128 * 384 * inner, bytes_accessed=32 << 20, transcendentals=0),
        name="attend",
    )(combo, half, qn, *own, *halos, masks)


def project_kernel(blocks, *refs):
    ins, w_ref, outs = refs[:blocks], refs[blocks], refs[blocks + 1 :]
    a = jnp.concatenate([i[...] for i in ins], axis=0)

    _, cores, zs, _, _ = w_ref.shape
    w = jnp.concatenate([w_ref[0, c, z] for z in range(zs) for c in range(cores)], axis=0)
    term = jnp.dot(a, w, preferred_element_type=F32)
    rows = outs[0].shape[0]
    for d, o in enumerate(outs):
        o[...] = term[d * rows : (d + 1) * rows, :].astype(BF16)


def project(blocks, weight, first, count):
    rows, depth = blocks[0].shape
    _, cores, zs, part, cols = weight.shape
    return pl.pallas_call(
        functools.partial(project_kernel, len(blocks)),
        grid=(count,),
        in_specs=[pl.BlockSpec((rows, depth), lambda j: (0, 0))] * len(blocks)
        + [pl.BlockSpec((1, cores, zs, part, cols), lambda j: (first + j, 0, 0, 0, 0))],
        out_specs=[pl.BlockSpec((rows, cols), lambda j: (0, j))] * len(blocks),
        out_shape=[jax.ShapeDtypeStruct((rows, count * cols), BF16)] * len(blocks),
        compiler_params=params(32),
        cost_estimate=pl.CostEstimate(
            flops=2 * len(blocks) * rows * depth * count * cols,
            bytes_accessed=2 * depth * count * cols,
            transcendentals=0,
        ),
        name="project",
    )(*blocks, in_hbm(weight))


def finish_kernel(y_ref, hidden, gate, mine, far0, pair0, across0, far1, pair1, across1, out):
    half, split = mine.shape[-1], far0.shape[-1]
    for first, last, far, pair, across in ((0, split, far0, pair0, across0), (split, half, far1, pair1, across1)):
        same = mine[:, first:last].astype(F32) + far[...].astype(F32)
        other = pair[...].astype(F32) + across[...].astype(F32)
        for side, branch in ((y_ref[0], same), (1 - y_ref[0], other)):
            where = pl.ds(pl.multiple_of(side * half + first, HEAD), last - first)
            out[:, where] = (hidden[:, where].astype(F32) + gate[:, where] * branch).astype(BF16)


def finish(y_lo, hidden, gate, pieces, blocks=4):
    rows, width = hidden.shape
    step = rows // blocks
    row_spec = pl.BlockSpec((step, width), lambda i, *_: (i, 0))
    return pl.pallas_call(
        finish_kernel,
        grid_spec=pltpu.PrefetchScalarGridSpec(
            num_scalar_prefetch=1,
            grid=(blocks,),
            in_specs=[row_spec, pl.BlockSpec((1, width), lambda i, *_: (0, 0))]
            + [pl.BlockSpec((step, p.shape[1]), lambda i, *_: (i, 0)) for p in pieces],
            out_specs=row_spec,
        ),
        out_shape=jax.ShapeDtypeStruct(hidden.shape, BF16),
        compiler_params=params(),
        name="finish",
    )(y_lo, hidden, gate[None], *pieces)


def shards(hidden_in, queries, keys, values, query_gain, key_gain, reach_time, reach_rows, reach_cols, out_weight, gate):
    frames, rows, nw, inner = queries.shape
    width = hidden_in.shape[3]
    weight = lax.all_gather(out_weight, "z", axis=0, tiled=False)
    tokens = [a.reshape(frames * rows, nw, inner) for a in (queries, keys, values)]
    qn, *own = prepare(*tokens, query_gain, key_gain)
    masks = mask_tables(
        lax.axis_index(TM) * frames,
        lax.axis_index(SP) * rows,
        frames * axis_size(TM),
        rows * axis_size(SP),
        nw,
    )
    combo = reach_time * 6 + reach_rows * 3 + reach_cols
    f0, f1, r0, r1 = own
    hb, ha = passed_along(f1, TM, 1), passed_along(f0, TM, -1)
    hb, ha, r0, r1, weight = lax.optimization_barrier((hb, ha, r0, r1, weight))
    weight = lax.all_gather(weight, ("x", "core"), axis=0, tiled=False)
    weight = weight.reshape((lax.axis_size("x"), lax.axis_size("core")) + weight.shape[1:])
    cb = passed_along(jnp.stack([hb[1], ha[1]]), SP, 1)
    ca = passed_along(jnp.stack([hb[0], ha[0]]), SP, -1)
    rb, ra = passed_along(r1, SP, 1), passed_along(r0, SP, -1)
    y_hi, y_lo = (lax.axis_index(a).astype(jnp.int32)[None] for a in ("y_hi", "y_lo"))
    same, other = attend(combo, y_hi, qn, (f0, f1), (hb, ha, rb, ra, cb, ca), masks)
    pair = [along_y(same, lambda y: y ^ 1), along_y(other, lambda y: 3 - y), along_y(other, lambda y: y ^ 2)]
    to_pair, to_across, to_far = project(pair, weight, 0, 2)
    large = [along_y(to_far, lambda y: y ^ 2), along_y(to_pair, lambda y: y ^ 1), along_y(to_across, lambda y: 3 - y)]
    pair[0], to_far = lax.optimization_barrier((pair[0], to_far))
    to_pair, to_across, to_far = project(pair, weight, 2, 2)
    same, to_far = lax.optimization_barrier((same, to_far))
    (mine,) = project([same], weight, 0, 4)
    to_across, large[1], large[2], mine = lax.optimization_barrier((to_across, large[1], large[2], mine))
    parts = [
        large,
        [along_y(to_far, lambda y: y ^ 2), along_y(to_pair, lambda y: y ^ 1), along_y(to_across, lambda y: 3 - y)],
    ]
    pieces = [mine] + parts[0] + parts[1]
    out = finish(y_lo, hidden_in.reshape(-1, width), gate, pieces)
    return out.reshape(hidden_in.shape)


def solution(mesh):
    inner_mesh = Mesh(mesh.devices.reshape(2, 4, 2, 8, 2), TM + SP)
    tokens = P(TM, SP, None, None)
    in_specs = (tokens,) * 4 + (P(),) * 5 + (P(SP, TM), P())
    return jax.shard_map(shards, mesh=inner_mesh, in_specs=in_specs, out_specs=tokens, check_vma=False)
```
